32 devices in a mesh: seq: 16 (over z, x, core), tp: 2 (over y).
Axes of the slice: x: 2, y: 2, z: 4, core: 2. Of those that a mesh axis runs over, the one named last changes fastest.
Arguments:
- tokens: bfloat16 [8192, 2560], P('seq', 'tp'), may hold values from -4 to 4
- norm_gain: bfloat16 [2560], P('tp'), may hold values from 0.099609375 to 1.8984375
- w_query: bfloat16 [2560, 2560], P(None, 'tp')
- w_key: bfloat16 [2560, 640], P(None, 'tp')
- w_value: bfloat16 [2560, 640], P(None, 'tp'), may hold values from -0.125 to 0.125
- w_out: bfloat16 [2560, 2560], P('tp'), may hold values from -0.125 to 0.125
- prior_cache: bfloat16 [512, 8, 2, 80, 128], P('seq', 'tp'), may hold values from -6 to 6
- prior_lens: int32 [16, 16], P('seq'), may hold values from 1 to 256, 2048 in all within a row
- span_lens: int32 [16, 16], P('seq'), may hold values from 1 to 64, 512 in all within a row
- prior_table: int32 [16, 16, 2], P('seq'), may hold values from 0 to 31, as said below
- dest_device: int32 [16, 16], P('seq'), may hold values from 0 to 15, each once within a row
- dest_table: int32 [16, 16, 2], P('seq'), may hold values from 0 to 31, as said below
Outputs:
- hidden: bfloat16 [8192, 2560], P('seq', 'tp')
- decode_cache: bfloat16 [512, 8, 2, 80, 128], P('seq', 'tp')
The draws below stay inside these ranges and needn't reach their ends.
Inputs may be any that keep to these rules, and one draw needn't show every extreme that they name: `prior_lens`: each row sums to 2048. `span_lens`: each row sums to 512. For each index s of seq, the entries prior_table[s] are a permutation of 0 to 31. `dest_device`: each row is a permutation of 0 to 15: every index of seq receives exactly one request from every index. For each receiving index d, the entries dest_table[d] are a permutation of 0 to 31.
All inputs are finite; a program needn't handle non-finite values.
Results may differ from the reference program's by a relative error of at most 0.0082.
Values may be sent and summed in bfloat16 or wider, within the bound.
No kernel may reach another device: no remote copies, remote signals or barrier semaphores. Data moves between devices by JAX's collectives and lax.ppermute only.
A program may use at most 128 MiB of HBM per device.

```python
import math
import jax
import jax.numpy as jnp
import numpy as np
from jax import lax

D = 2560
HEADS = 32
KV_HEADS = 8
HEAD_DIM = 80
BT = 128
PB = 2
TOK_DEV = 512
QMAX = 64
REQ_DEV = 16
POOL = 32
DSLOTS = 32
TOKENS = 8192
N_SEQ = 16


def plant_parts(key):
    base_key = jax.random.fold_in(key, 101)
    signs = jnp.where(jax.random.bernoulli(jax.random.fold_in(base_key, 1), 0.5, (D,)), 1.0, -1.0).astype(jnp.float32)
    group = jax.random.randint(jax.random.fold_in(base_key, 2), (), 0, KV_HEADS)
    return (signs, group)


def planted_columns(signs, group, base, columns, group_cols):
    column_ids = jnp.arange(columns, dtype=jnp.int32)
    is_plant = (column_ids % HEAD_DIM == HEAD_DIM - 1) & (column_ids // HEAD_DIM // group_cols == group)
    return jnp.where(is_plant[None, :], 1.25 * signs[:, None], base) / math.sqrt(D)


def draw_tokens(key, part):
    signs, group = plant_parts(key)
    noise = jnp.clip(jax.random.normal(jax.random.fold_in(key, 41), (TOKENS, D), jnp.float32), -4.0, 4.0)
    drawn = noise
    pair_pick = jax.random.randint(jax.random.fold_in(key, 44), (TOKENS // 2,), 0, 16) == 0
    picked = jnp.repeat(pair_pick, 2)
    strength = jnp.repeat(jax.random.uniform(jax.random.fold_in(key, 45), (TOKENS // 2,), jnp.float32, 0.7, 0.95), 2)
    remainder = jnp.sqrt(1.0 - strength * strength)
    planted = strength[:, None] * signs[None, :] + remainder[:, None] * noise
    return jnp.where(picked[:, None], planted, drawn).astype(jnp.bfloat16)


def draw_w_query(key, part):
    signs, group = plant_parts(key)
    columns = HEADS * HEAD_DIM
    base = jnp.clip(jax.random.normal(jax.random.fold_in(key, 51), (D, columns), jnp.float32), -4.0, 4.0)
    return planted_columns(signs, group, base, columns, HEADS // KV_HEADS).astype(jnp.bfloat16)


def draw_w_key(key, part):
    signs, group = plant_parts(key)
    columns = KV_HEADS * HEAD_DIM
    base = jnp.clip(jax.random.normal(jax.random.fold_in(key, 61), (D, columns), jnp.float32), -4.0, 4.0)
    return planted_columns(signs, group, base, columns, 1).astype(jnp.bfloat16)


def draw_prior_table(key, part):
    keys = jax.random.split(jax.random.fold_in(key, 11), N_SEQ)
    perms = jax.vmap(lambda k: jax.random.permutation(k, REQ_DEV * PB))(keys)
    return perms.reshape(N_SEQ, REQ_DEV, PB).astype(jnp.int32)


def draw_dest_table(key, part):
    keys = jax.random.split(jax.random.fold_in(key, 23), N_SEQ)
    perms = jax.vmap(lambda k: jax.random.permutation(k, N_SEQ * PB))(keys)
    return perms.reshape(N_SEQ, N_SEQ, PB).astype(jnp.int32)


def block_scale(stream_key, extent, shards, smallest, high):
    loudness = 1.0
    for dim, blocks in shards:
        draws = jax.random.uniform(jax.random.fold_in(jax.random.fold_in(stream_key, 6), dim), (blocks,), jnp.float32, smallest / len(shards), high / len(shards))
        loudness = loudness * jnp.repeat(jnp.exp(draws), extent[dim] // blocks).reshape((-1,) + (1,) * (len(extent) - 1 - dim))
    return loudness


def profile(amount, total, limit, skew):
    portions = [(1 << 20) // math.isqrt(grade ** skew) + 1 for grade in range(2, amount + 1)]
    surplus, counts = total - limit - (amount - 1), [1] * (amount - 1)
    while surplus > 0:
        candidates = [i for i in range(amount - 1) if counts[i] < limit]
        mass, left = sum([portions[i] for i in candidates]), surplus
        for i in candidates:
            more = min(limit - counts[i], max(1, left * portions[i] // mass), surplus)
            counts[i] = counts[i] + more
            surplus = surplus - more
    return np.array([limit] + counts)


def ragged_sizes(stream_key, amount, total, bound, slope):
    if amount == 2:
        one = jax.random.randint(stream_key, (), max(1, total - bound), min(bound, total - 1) + 1)
        return jnp.stack([one, total - one])
    tallies = jnp.asarray(profile(amount, total, bound, slope), jnp.int32)
    pairs = (amount - 1) // 2
    donor, receiver = tallies[1:1 + 2 * pairs:2], tallies[2:2 + 2 * pairs:2]
    room = jnp.minimum(donor - 1, bound - receiver)
    shifted = jax.random.randint(jax.random.fold_in(stream_key, 1), (pairs,), 0, 1 << 20) % (room + 1)
    tallies = tallies.at[1:1 + 2 * pairs:2].set(donor - shifted).at[2:2 + 2 * pairs:2].set(receiver + shifted)
    return tallies[jax.random.permutation(jax.random.fold_in(stream_key, 2), amount)]


def centred(own_key, extent, spread, limit, cuts=(), kind=jnp.bfloat16):
    factor_of = block_scale(own_key, extent, cuts, -0.22, 0.18) if cuts else 1.0
    drawn = jax.random.normal(own_key, extent, jnp.float32) * spread * factor_of
    return jnp.minimum(jnp.maximum(drawn, -limit), limit).astype(kind)


def setup_inputs(seed: int = 0) -> dict:
    streams_of = jax.random.split(jax.random.key(seed), 13)
    return {
        "tokens": draw_tokens(jax.random.fold_in(streams_of[12], 71), 0),
        "norm_gain": jnp.clip(1.0 + 0.18 * jax.random.normal(streams_of[1], (D,), jnp.float32), 0.099609375, 1.8984375).astype(jnp.bfloat16),
        "w_query": draw_w_query(jax.random.fold_in(streams_of[12], 71), 0),
        "w_key": draw_w_key(jax.random.fold_in(streams_of[12], 71), 0),
        "w_value": centred(streams_of[4], (D, KV_HEADS * HEAD_DIM), D ** -0.5, 0.125, ((1, 2),)),
        "w_out": centred(streams_of[5], (HEADS * HEAD_DIM, D), (HEADS * HEAD_DIM) ** -0.5, 0.125, ((0, 2),)),
        "prior_cache": centred(streams_of[6], (N_SEQ * POOL, KV_HEADS, 2, HEAD_DIM, BT), 1.0, 6.0, ((0, 16), (1, 2))),
        "prior_lens": jax.vmap(lambda own: ragged_sizes(own, REQ_DEV, REQ_DEV * PB * BT // 2, PB * BT, 2))(jax.random.split(streams_of[7], N_SEQ)).reshape((N_SEQ, REQ_DEV)).astype(jnp.int32),
        "span_lens": jax.vmap(lambda own: ragged_sizes(own, REQ_DEV, TOK_DEV, QMAX, 2))(jax.random.split(streams_of[8], N_SEQ)).reshape((N_SEQ, REQ_DEV)).astype(jnp.int32),
        "prior_table": draw_prior_table(jax.random.fold_in(streams_of[12], 71), 0),
        "dest_device": jax.vmap(lambda own: jax.random.permutation(own, N_SEQ))(jax.random.split(streams_of[10], N_SEQ)).reshape((N_SEQ, REQ_DEV)).astype(jnp.int32),
        "dest_table": draw_dest_table(jax.random.fold_in(streams_of[12], 71), 0),
    }


EPS = 1e-05
THETA = 1000000.0
MASKED = -1e+30

def rotate(values_in, positions):
    half_dim = values_in.shape[-1] // 2
    freq_index = jnp.arange(half_dim, dtype=jnp.float32)
    inverse = THETA ** (-2.0 * freq_index / values_in.shape[-1])
    angles = positions.astype(jnp.float32)[:, None] * inverse[None, :]
    cosine_part = jnp.cos(angles)[:, None, :]
    sine_part = jnp.sin(angles)[:, None, :]
    lower_half = values_in[..., :half_dim]
    upper_half = values_in[..., half_dim:]
    return jnp.concatenate([lower_half * cosine_part - upper_half * sine_part, upper_half * cosine_part + lower_half * sine_part], axis=-1)

def attend(query, key_new, value_new, block_pool, prior_row, span_row, slot_table, head_dim):
    tok_rows = query.shape[0]
    q_heads = query.shape[1] // head_dim
    kv_heads = key_new.shape[1] // head_dim
    group_size = q_heads // kv_heads
    window_rows = tok_rows // 8
    blocks_per = slot_table.shape[1]
    block_len = block_pool.shape[-1]
    offsets = (jnp.cumsum(span_row) - span_row).astype(jnp.int32)
    token_pos = jnp.arange(tok_rows, dtype=jnp.int32)
    segment = (lax.optimization_barrier(jnp.sum((token_pos[:, None] >= offsets[None, :]).astype(jnp.int32), axis=1)) - 1).astype(jnp.int32)
    within = (token_pos - jnp.take(offsets, segment)).astype(jnp.int32)
    positions = jnp.take(prior_row, segment) + within
    query = rotate(query.reshape(tok_rows, q_heads, head_dim), positions).astype(jnp.bfloat16)
    key_new = rotate(key_new.reshape(tok_rows, kv_heads, head_dim), positions).astype(jnp.bfloat16)
    value_new = value_new.reshape(tok_rows, kv_heads, head_dim)
    padded_q = jnp.concatenate([query, jnp.zeros((window_rows, q_heads, head_dim), jnp.bfloat16)], axis=0)
    padded_k = jnp.concatenate([key_new, jnp.zeros((window_rows, kv_heads, head_dim), jnp.bfloat16)], axis=0)
    padded_v = jnp.concatenate([value_new, jnp.zeros((window_rows, kv_heads, head_dim), jnp.bfloat16)], axis=0)
    score_scale = 1.0 / math.sqrt(head_dim)
    old_pos = jnp.arange(blocks_per * block_len, dtype=jnp.int32)
    query_pos = jnp.arange(window_rows, dtype=jnp.int32)

    def per_request(offset, span_len, prior_len, slot_ids):
        rows_q = lax.dynamic_slice_in_dim(padded_q, offset, window_rows, 0).astype(jnp.float32).reshape(window_rows, kv_heads, group_size, head_dim)
        rows_k = lax.dynamic_slice_in_dim(padded_k, offset, window_rows, 0).astype(jnp.float32)
        rows_v = lax.dynamic_slice_in_dim(padded_v, offset, window_rows, 0).astype(jnp.float32)
        blocks = jnp.take(block_pool, slot_ids, axis=0)
        keys_old = jnp.transpose(blocks[:, :, 0], (1, 2, 0, 3)).reshape(kv_heads, head_dim, blocks_per * block_len).astype(jnp.float32)
        values_old = jnp.transpose(blocks[:, :, 1], (1, 2, 0, 3)).reshape(kv_heads, head_dim, blocks_per * block_len).astype(jnp.float32)
        score_old = jnp.einsum('qkgd,kdt->kgqt', rows_q, keys_old) * score_scale
        score_new = jnp.einsum('qkgd,pkd->kgqp', rows_q, rows_k) * score_scale
        old_ok = old_pos < prior_len
        new_ok = (query_pos[None, :] <= query_pos[:, None]) & (query_pos[None, :] < span_len)
        score_old = jnp.where(old_ok[None, None, None, :], score_old, MASKED)
        score_new = jnp.where(new_ok[None, None, :, :], score_new, MASKED)
        highest = jnp.maximum(lax.optimization_barrier(jnp.max(score_old, axis=-1)), lax.optimization_barrier(jnp.max(score_new, axis=-1)))[..., None]
        exp_old = jnp.exp(score_old - highest)
        exp_new = jnp.exp(score_new - highest)
        denominator = lax.optimization_barrier(jnp.sum(exp_old, axis=-1, keepdims=True)) + lax.optimization_barrier(jnp.sum(exp_new, axis=-1, keepdims=True))
        prob_old = lax.optimization_barrier((exp_old / denominator).astype(jnp.bfloat16)).astype(jnp.float32)
        prob_new = lax.optimization_barrier((exp_new / denominator).astype(jnp.bfloat16)).astype(jnp.float32)
        mixed_rows = jnp.einsum('kgqt,kdt->qkgd', prob_old, values_old) + jnp.einsum('kgqp,pkd->qkgd', prob_new, rows_v)
        return mixed_rows.reshape(window_rows, q_heads * head_dim).astype(jnp.bfloat16)
    results = jax.vmap(per_request)(offsets, span_row, prior_row, slot_table)
    flat_rows = results.reshape(results.shape[0] * window_rows, q_heads * head_dim)
    picked = (segment * window_rows + within).astype(jnp.int32)
    return jnp.take(flat_rows, picked, axis=0)

def reference(tokens, norm_gain, w_query, w_key, w_value, w_out, prior_cache, prior_lens, span_lens, prior_table, dest_device, dest_table):
    gain_wide = norm_gain.astype(jnp.float32)
    source = prior_cache.reshape(N_SEQ, POOL, KV_HEADS, 2, HEAD_DIM, BT)

    def device_block(operand):
        row_block, prior_row, span_row, slot_table, block_pool = operand
        widened = row_block.astype(jnp.float32)
        mean_sq = lax.optimization_barrier(jnp.mean(widened * widened, axis=1, keepdims=True))
        normed = (widened * lax.rsqrt(mean_sq + EPS) * gain_wide[None, :]).astype(jnp.bfloat16)
        query = jnp.dot(normed, w_query, preferred_element_type=jnp.float32)
        key_new = jnp.dot(normed, w_key, preferred_element_type=jnp.float32)
        value_new = jnp.dot(normed, w_value, preferred_element_type=jnp.float32).astype(jnp.bfloat16)
        attended = attend(query, key_new, value_new, block_pool, prior_row, span_row, slot_table, HEAD_DIM)
        projected = jnp.dot(attended, w_out, preferred_element_type=jnp.float32)
        return (widened + projected).astype(jnp.bfloat16)
    hidden = lax.map(device_block, (tokens.reshape(N_SEQ, TOK_DEV, D), prior_lens, span_lens, prior_table, source)).reshape(TOKENS, D)
    blocks = jax.vmap(lambda block_pool, slot_table: jnp.take(block_pool, slot_table.reshape(-1), axis=0))(source, prior_table)
    blocks = blocks.reshape(N_SEQ, REQ_DEV, PB, KV_HEADS, 2, HEAD_DIM, BT)
    token_pos = (jnp.arange(PB, dtype=jnp.int32)[:, None] * BT + jnp.arange(BT, dtype=jnp.int32)[None, :]).astype(jnp.int32)
    in_range = token_pos[None, None, :, :] < prior_lens[:, :, None, None]
    blocks = jnp.where(in_range[:, :, :, None, None, None, :], blocks, jnp.zeros((), jnp.bfloat16))
    sender = jnp.arange(N_SEQ, dtype=jnp.int32)[:, None, None]
    block_index = jnp.arange(PB, dtype=jnp.int32)[None, None, :]
    dest_dev = dest_device[:, :, None]
    dest_slot = (dest_dev * DSLOTS + dest_table[dest_dev, sender, block_index]).astype(jnp.int32)
    decode_cache = jnp.zeros((N_SEQ * DSLOTS, KV_HEADS, 2, HEAD_DIM, BT), jnp.bfloat16)
    decode_cache = decode_cache.at[dest_slot.reshape(-1)].set(blocks.reshape(N_SEQ * REQ_DEV * PB, KV_HEADS, 2, HEAD_DIM, BT))
    return (hidden, decode_cache)
```

```python
import functools
import math

import jax
import jax.numpy as jnp
import numpy as np
from jax import lax
from jax.experimental import pallas as pl
from jax.experimental.pallas import tpu as pltpu
from jax.sharding import PartitionSpec as P

HEAD_DIM = 80
HALF = HEAD_DIM // 2
LANES = 128
WINDOW = 64
EPS = 1e-05
THETA = 1000000.0
MASKED = -1e30
ROWS = 32
NT = (((1,), (1,)), ((), ()))


def smem():
    return pl.BlockSpec(memory_space=pltpu.SMEM)


def vmem():
    return pl.BlockSpec(memory_space=pltpu.VMEM)


def hbm():
    return pl.BlockSpec(memory_space=pl.ANY)


def pack_body(dest_ref, lens_ref, table_ref, cache_ref, out_ref, buf, sem_in, sem_out):
    reqs = dest_ref.shape[1]
    per = table_ref.shape[2]
    block_len = cache_ref.shape[-1]

    def valid(r, j):
        return lens_ref[0, r] - j * block_len

    def fetch(r, j):
        return pltpu.make_async_copy(
            cache_ref.at[table_ref[0, r, j]], buf.at[r * per + j], sem_in.at[r * per + j]
        )

    def ship(r, j):
        return pltpu.make_async_copy(
            buf.at[r * per + j], out_ref.at[dest_ref[0, r], j], sem_out.at[r * per + j]
        )

    def start(r, carry):
        for j in range(per):
            @pl.when(valid(r, j) > 0)
            def _():
                fetch(r, j).start()
        return carry

    def finish(r, carry):
        for j in range(per):
            count = valid(r, j)

            @pl.when(count > 0)
            def _():
                fetch(r, j).wait()

            @pl.when(count < block_len)
            def _():
                block = buf[r * per + j]
                lane = lax.broadcasted_iota(jnp.int32, block.shape, block.ndim - 1)
                buf[r * per + j] = jnp.where(
                    (lane < count) & (count > 0), block.astype(jnp.float32), 0.0
                ).astype(jnp.bfloat16)

            ship(r, j).start()
        return carry

    def drain(r, carry):
        for j in range(per):
            ship(r, j).wait()
        return carry

    lax.fori_loop(0, reqs, start, 0)
    lax.fori_loop(0, reqs, finish, 0)
    lax.fori_loop(0, reqs, drain, 0)


def pack(dest, lens, table, cache):
    reqs, per = table.shape[1], table.shape[2]
    count = reqs * per
    return pl.pallas_call(
        pack_body,
        out_shape=jax.ShapeDtypeStruct((reqs, per) + cache.shape[1:], cache.dtype),
        in_specs=[smem(), smem(), smem(), hbm()],
        out_specs=hbm(),
        scratch_shapes=[
            pltpu.VMEM((count,) + cache.shape[1:], cache.dtype),
            pltpu.SemaphoreType.DMA((count,)),
            pltpu.SemaphoreType.DMA((count,)),
        ],
        compiler_params=pltpu.CompilerParams(vmem_limit_bytes=16 << 20),
        name="pack",
    )(dest, lens, table, cache)


def place_body(table_ref, in_ref, out_ref, sem):
    peers, per = table_ref.shape[1], table_ref.shape[2]

    def move(s, j):
        return pltpu.make_async_copy(
            in_ref.at[s, j], out_ref.at[table_ref[0, s, j]], sem.at[s * per + j]
        )

    def start(s, carry):
        for j in range(per):
            move(s, j).start()
        return carry

    def drain(s, carry):
        for j in range(per):
            move(s, j).wait()
        return carry

    lax.fori_loop(0, peers, start, 0)
    lax.fori_loop(0, peers, drain, 0)


def place(table, incoming):
    peers, per = incoming.shape[:2]
    return pl.pallas_call(
        place_body,
        out_shape=jax.ShapeDtypeStruct((peers * per,) + incoming.shape[2:], incoming.dtype),
        in_specs=[smem(), hbm()],
        out_specs=hbm(),
        scratch_shapes=[pltpu.SemaphoreType.DMA((peers * per,))],
        name="place",
    )(table, incoming)


def layer_body(ways, q_heads, kv_heads, *refs):
    (span_ref, lens_ref, table_ref, inv_ref) = refs[:4]
    gains = refs[4 : 4 + ways]
    xs = refs[4 + ways : 4 + 2 * ways]
    wq_ref, wk_ref, wv_ref, wo_ref, cache_ref = refs[4 + 2 * ways : 9 + 2 * ways]
    base_ref = refs[9 + 2 * ways]
    sends = refs[10 + 2 * ways : 9 + 3 * ways]
    (
        x_s, nrm_s, wq_s, wk_s, wv_s, wo_s, kv_s, acc_s, q_s, k_s, v_s, att_s, flat_s,
        cos_s, low_s, high_s, x_sem, w_sem, o_sem, kv_sem,
    ) = refs[9 + 3 * ways :]
    rows, feats = xs[0].shape
    reqs, per = table_ref.shape[1], table_ref.shape[2]
    block_len = cache_ref.shape[-1]
    group = q_heads // kv_heads
    me = lax.axis_index("tp")

    def x_copy(t):
        return pltpu.make_async_copy(xs[t], x_s.at[t], x_sem.at[t])

    w_copies = [
        pltpu.make_async_copy(wq_ref, wq_s, w_sem.at[0]),
        pltpu.make_async_copy(wk_ref, wk_s, w_sem.at[1]),
        pltpu.make_async_copy(wv_ref, wv_s, w_sem.at[2]),
    ]

    def o_copy(t):
        col = pl.multiple_of(lax.rem(me + t, ways) * feats, LANES)
        return pltpu.make_async_copy(wo_ref.at[:, pl.ds(col, feats)], wo_s.at[t], o_sem.at[t])

    def kv_copy(r, j):
        return pltpu.make_async_copy(
            cache_ref.at[table_ref[0, r, j]],
            kv_s.at[r, :, :, pl.ds(0, HEAD_DIM), pl.ds(j * block_len, block_len)],
            kv_sem.at[r * per + j],
        )

    for t in range(ways):
        x_copy(t).start()
    for copy in w_copies:
        copy.start()

    def kv_start(r, carry):
        for j in range(per):
            kv_copy(r, j).start()
        return carry

    lax.fori_loop(0, reqs, kv_start, 0)
    for t in range(ways):
        o_copy(t).start()

    row_id = lax.broadcasted_iota(jnp.int32, (rows, LANES), 0)

    def shift_of(r, carry):
        offset, shift = carry
        shift = jnp.where(row_id >= offset, lens_ref[0, r] - offset, shift)
        return offset + span_ref[0, r], shift

    _, shift = lax.fori_loop(0, reqs, shift_of, (jnp.int32(0), jnp.zeros_like(row_id)))
    angle = (row_id + shift).astype(jnp.float32) * inv_ref[...]
    lane = lax.broadcasted_iota(jnp.int32, (rows, LANES), 1)
    cos_s[...] = jnp.where(lane < HEAD_DIM, jnp.cos(angle), 0.0)
    sine = jnp.sin(angle)
    low_s[...] = jnp.where(lane < HALF, -sine, 0.0)
    high_s[...] = jnp.where((lane >= HALF) & (lane < HEAD_DIM), sine, 0.0)

    pad = kv_s.shape[3] - HEAD_DIM
    zeros_kv = jnp.zeros((2, pad, kv_s.shape[4]), kv_s.dtype)

    def kv_zero(r, carry):
        for g in range(kv_heads):
            kv_s[r, g, :, HEAD_DIM:, :] = zeros_kv
        return carry

    lax.fori_loop(0, reqs, kv_zero, 0)
    acc_s[...] = jnp.zeros(acc_s.shape, acc_s.dtype)
    att_s[...] = jnp.zeros(att_s.shape, att_s.dtype)

    for t in range(ways):
        x_copy(t).wait()
    step = 64

    def norm_rows(m, carry):
        here = pl.ds(pl.multiple_of(m * step, step), step)
        wide = [x_s[t, here, :].astype(jnp.float32) for t in range(ways)]
        total = sum(jnp.sum(w * w, axis=1, keepdims=True) for w in wide)
        scale = lax.rsqrt(total / (ways * feats) + EPS)
        for t in range(ways):
            nrm_s[lax.rem(me + t, ways), here, :] = (
                wide[t] * scale * gains[t][...].astype(jnp.float32)
            ).astype(jnp.bfloat16)
        return carry

    lax.fori_loop(0, rows // step, norm_rows, 0)

    tall = 256

    def project(w_s, first, width, here):
        total = None
        for c in range(ways):
            part = jnp.dot(
                nrm_s[c, here, :],
                w_s[c * feats : (c + 1) * feats, first : first + width],
                preferred_element_type=jnp.float32,
            )
            total = part if total is None else total + part
        acc_s[:, :width] = total

    def head_of(h):
        base = HEAD_DIM * h // LANES * LANES
        shift = HEAD_DIM * h - base
        wide = acc_s[:, base : base + 2 * LANES]
        if shift:
            wide = pltpu.roll(wide, 2 * LANES - shift, 1)
        return wide[:, :LANES]

    def rotated(h, here):
        value = head_of(h)
        return (
            value * cos_s[here, :]
            + pltpu.roll(value, LANES - HALF, 1) * low_s[here, :]
            + pltpu.roll(value, HALF, 1) * high_s[here, :]
        ).astype(jnp.bfloat16)

    for copy in w_copies:
        copy.wait()
    block_heads = min(8, q_heads)

    def project_rows(m, carry):
        here = pl.ds(pl.multiple_of(m * tall, tall), tall)
        project(wk_s, 0, kv_heads * HEAD_DIM, here)
        for g in range(kv_heads):
            k_s[g, here, :] = rotated(g, here)
        project(wv_s, 0, kv_heads * HEAD_DIM, here)
        narrow = lax.broadcasted_iota(jnp.int32, (tall, LANES), 1) < HEAD_DIM
        for g in range(kv_heads):
            v_s[g, here, :] = jnp.where(narrow, head_of(g), 0.0).astype(jnp.bfloat16)
        for block in range(q_heads // block_heads):
            project(wq_s, block * block_heads * HEAD_DIM, block_heads * HEAD_DIM, here)
            for h in range(block_heads):
                q_s[block * block_heads + h, here, :] = rotated(h, here)
        return carry

    lax.fori_loop(0, rows // tall, project_rows, 0)

    log_scale = (1.0 / math.sqrt(HEAD_DIM)) * math.log2(math.e)
    keys_old = per * block_len

    def request(r, offset):
        span = span_ref[0, r]
        prior = lens_ref[0, r]
        for j in range(per):
            kv_copy(r, j).wait()
        first = offset // 16 * 16
        key_first = pl.multiple_of(jnp.minimum(first, rows - LANES), 16)
        old_ok = lax.broadcasted_iota(jnp.int32, (1, keys_old), 1) < prior

        def tile(i, carry):
            begin = pl.multiple_of(first + i * ROWS, 16)
            here = pl.ds(begin, ROWS)
            row = begin + lax.broadcasted_iota(jnp.int32, (ROWS, LANES), 0)
            key = key_first + lax.broadcasted_iota(jnp.int32, (ROWS, LANES), 1)
            new_ok = ((key <= row) & (key >= offset))[None]
            keep = ((row >= offset) & (row < offset + span))[None]
            for g in range(kv_heads):
                heads = slice(g * group, (g + 1) * group)
                query = q_s[heads, here, :].reshape(group * ROWS, LANES)
                old = jnp.dot(query, kv_s[r, g, 0], preferred_element_type=jnp.float32)
                new = lax.dot_general(
                    query, k_s[g, pl.ds(key_first, LANES), :], NT,
                    preferred_element_type=jnp.float32,
                )
                old = jnp.where(old_ok, old, MASKED)
                new = jnp.where(new_ok, new.reshape(group, ROWS, LANES), MASKED)
                new = new.reshape(group * ROWS, LANES)
                top = jnp.maximum(
                    jnp.max(old, axis=1, keepdims=True), jnp.max(new, axis=1, keepdims=True)
                )
                old = jnp.exp2((old - top) * log_scale)
                new = jnp.exp2((new - top) * log_scale)
                total = jnp.sum(old, axis=1, keepdims=True) + jnp.sum(new, axis=1, keepdims=True)
                mixed = lax.dot_general(
                    old.astype(jnp.bfloat16), kv_s[r, g, 1], NT,
                    preferred_element_type=jnp.float32,
                ) + jnp.dot(
                    new.astype(jnp.bfloat16), v_s[g, pl.ds(key_first, LANES), :],
                    preferred_element_type=jnp.float32,
                )
                mixed = (mixed / total).reshape(group, ROWS, LANES)
                att_s[heads, here, :] = jnp.where(keep, mixed, att_s[heads, here, :])
            return carry

        lax.fori_loop(0, (offset - first + span + ROWS - 1) // ROWS, tile, 0)
        return offset + span

    lax.fori_loop(0, reqs, request, jnp.int32(0))

    for t in range(ways):
        o_copy(t).wait()

    def out_rows(m, carry):
        here = pl.ds(pl.multiple_of(m * tall, tall), tall)
        flat_s[...] = jnp.zeros(flat_s.shape, flat_s.dtype)
        for h in range(q_heads):
            base = HEAD_DIM * h // LANES * LANES
            shift = HEAD_DIM * h - base
            value = att_s[h, here, :]
            wide = jnp.concatenate([value, jnp.zeros_like(value)], axis=1)
            if shift:
                wide = pltpu.roll(wide, shift, 1)
            flat_s[:, base : base + 2 * LANES] += wide
        flat = flat_s[:, : q_heads * HEAD_DIM].astype(jnp.bfloat16)
        for t in range(ways):
            part = jnp.dot(flat, wo_s[t], preferred_element_type=jnp.float32)
            if t == 0:
                base_ref[here, :] = x_s[0, here, :].astype(jnp.float32) + part
            else:
                sends[t - 1][here, :] = part.astype(jnp.bfloat16)
        return carry

    lax.fori_loop(0, rows // tall, out_rows, 0)


def layer(ways, spans, lens, table, gains, xs, w_query, w_key, w_value, w_out, cache):
    rows, feats = xs[0].shape
    q_heads = w_query.shape[1] // HEAD_DIM
    kv_heads = w_key.shape[1] // HEAD_DIM
    reqs, per = table.shape[1], table.shape[2]
    keys = per * cache.shape[-1]
    pairs = np.arange(LANES) % HALF
    inverse = np.where(
        np.arange(LANES) < HEAD_DIM, np.float64(THETA) ** (-2.0 * pairs / HEAD_DIM), 0.0
    ).astype(np.float32)[None]
    bf, f32 = jnp.bfloat16, jnp.float32
    outs = pl.pallas_call(
        functools.partial(layer_body, ways, q_heads, kv_heads),
        out_shape=[jax.ShapeDtypeStruct((rows, feats), f32)]
        + [jax.ShapeDtypeStruct((rows, feats), bf)] * (ways - 1),
        in_specs=[smem(), smem(), smem(), vmem()] + [vmem()] * ways + [hbm()] * (ways + 5),
        out_specs=[vmem()] * ways,
        scratch_shapes=[
            pltpu.VMEM((ways, rows, feats), bf),
            pltpu.VMEM((ways, rows, feats), bf),
            pltpu.VMEM(w_query.shape, bf),
            pltpu.VMEM(w_key.shape, bf),
            pltpu.VMEM(w_value.shape, bf),
            pltpu.VMEM((ways, w_out.shape[0], feats), bf),
            pltpu.VMEM((reqs, kv_heads, 2, LANES, keys), bf),
            pltpu.VMEM((256, min(8, q_heads) * HEAD_DIM + LANES), f32),
            pltpu.VMEM((q_heads, rows + ROWS, LANES), bf),
            pltpu.VMEM((kv_heads, rows, LANES), bf),
            pltpu.VMEM((kv_heads, rows, LANES), bf),
            pltpu.VMEM((q_heads, rows + ROWS, LANES), f32),
            pltpu.VMEM((256, q_heads * HEAD_DIM + LANES), f32),
            pltpu.VMEM((rows, LANES), f32),
            pltpu.VMEM((rows, LANES), f32),
            pltpu.VMEM((rows, LANES), f32),
            pltpu.SemaphoreType.DMA((ways,)),
            pltpu.SemaphoreType.DMA((3,)),
            pltpu.SemaphoreType.DMA((ways,)),
            pltpu.SemaphoreType.DMA((reqs * per,)),
        ],
        compiler_params=pltpu.CompilerParams(vmem_limit_bytes=58 << 20),
        name="layer",
    )(spans, lens, table, jnp.asarray(inverse), *gains, *xs, w_query, w_key, w_value, w_out, cache)
    return outs[0], outs[1:]


def local(
    tokens,
    norm_gain,
    w_query,
    w_key,
    w_value,
    w_out,
    prior_cache,
    prior_lens,
    span_lens,
    prior_table,
    dest_device,
    dest_table,
):
    ways = lax.axis_size("tp")
    gain = norm_gain[None, :]

    def from_peer(value, t):
        return lax.ppermute(value, "tp", [((d + t) % ways, d) for d in range(ways)])

    def to_peer(value, t):
        return lax.ppermute(value, "tp", [(d, (d + t) % ways) for d in range(ways)])

    outgoing = pack(dest_device, prior_lens, prior_table, prior_cache)
    incoming = lax.all_to_all(outgoing, "seq", split_axis=0, concat_axis=0, tiled=True)
    xs = [tokens] + [from_peer(tokens, t) for t in range(1, ways)]
    gains = [gain] + [from_peer(gain, t) for t in range(1, ways)]
    base, sends = layer(
        ways, span_lens, prior_lens, prior_table, gains, xs,
        w_query, w_key, w_value, w_out, prior_cache,
    )
    total = base
    for t in range(1, ways):
        total = total + to_peer(sends[t - 1], t).astype(jnp.float32)
    hidden = total.astype(jnp.bfloat16)
    decode_cache = place(dest_table, incoming)
    return (hidden, decode_cache)


def solution(mesh):
    in_specs = (
        P("seq", "tp"),
        P("tp"),
        P(None, "tp"),
        P(None, "tp"),
        P(None, "tp"),
        P("tp", None),
        P("seq", "tp", None, None, None),
        P("seq", None),
        P("seq", None),
        P("seq", None, None),
        P("seq", None),
        P("seq", None, None),
    )
    out_specs = (P("seq", "tp"), P("seq", "tp", None, None, None))
    return jax.shard_map(local, mesh=mesh, in_specs=in_specs, out_specs=out_specs, check_vma=False)
```

```python
import functools
import math

import jax
import jax.numpy as jnp
import numpy as np
from jax import lax
from jax.experimental import pallas as pl
from jax.experimental.pallas import tpu as pltpu
from jax.sharding import PartitionSpec as P

HEAD_DIM = 80
HALF = HEAD_DIM // 2
LANES = 128
WINDOW = 64
EPS = 1e-05
THETA = 1000000.0
MASKED = -1e30
ROWS = 32
NT = (((1,), (1,)), ((), ()))


def smem():
    return pl.BlockSpec(memory_space=pltpu.SMEM)


def vmem():
    return pl.BlockSpec(memory_space=pltpu.VMEM)


def hbm():
    return pl.BlockSpec(memory_space=pl.ANY)


def pack_body(dest_ref, lens_ref, table_ref, cache_ref, out_ref, buf, sem_in, sem_out):
    reqs = dest_ref.shape[1]
    per = table_ref.shape[1]
    block_len = cache_ref.shape[-1]

    def valid(r, j):
        return lens_ref[0, r] - j * block_len

    def fetch(r, j):
        return pltpu.make_async_copy(
            cache_ref.at[table_ref[0, j, r]], buf.at[r * per + j], sem_in.at[r * per + j]
        )

    def ship(r, j):
        return pltpu.make_async_copy(
            buf.at[r * per + j], out_ref.at[dest_ref[0, r], j], sem_out.at[r * per + j]
        )

    def start(r, carry):
        for j in range(per):
            @pl.when(valid(r, j) > 0)
            def _():
                fetch(r, j).start()
        return carry

    def finish(r, carry):
        for j in range(per):
            count = valid(r, j)

            @pl.when(count > 0)
            def _():
                fetch(r, j).wait()

            @pl.when(count < block_len)
            def _():
                block = buf[r * per + j]
                lane = lax.broadcasted_iota(jnp.int32, block.shape, block.ndim - 1)
                buf[r * per + j] = jnp.where(
                    (lane < count) & (count > 0), block.astype(jnp.float32), 0.0
                ).astype(jnp.bfloat16)

            ship(r, j).start()
        return carry

    def drain(r, carry):
        for j in range(per):
            ship(r, j).wait()
        return carry

    lax.fori_loop(0, reqs, start, 0)
    lax.fori_loop(0, reqs, finish, 0)
    lax.fori_loop(0, reqs, drain, 0)


def pack(dest, lens, table, cache):
    per, reqs = table.shape[1], table.shape[2]
    count = reqs * per
    return pl.pallas_call(
        pack_body,
        out_shape=jax.ShapeDtypeStruct((reqs, per) + cache.shape[1:], cache.dtype),
        in_specs=[smem(), smem(), smem(), hbm()],
        out_specs=hbm(),
        scratch_shapes=[
            pltpu.VMEM((count,) + cache.shape[1:], cache.dtype),
            pltpu.SemaphoreType.DMA((count,)),
            pltpu.SemaphoreType.DMA((count,)),
        ],
        compiler_params=pltpu.CompilerParams(vmem_limit_bytes=60 << 20),
        name="pack",
    )(dest, lens, table, cache)


def place_body(table_ref, in_ref, out_ref, buf, sem_in, sem_out):
    per, peers = table_ref.shape[1], table_ref.shape[2]

    def fetch(s, j):
        return pltpu.make_async_copy(
            in_ref.at[s, j], buf.at[s * per + j], sem_in.at[s * per + j]
        )

    def ship(s, j):
        return pltpu.make_async_copy(
            buf.at[s * per + j], out_ref.at[table_ref[0, j, s]], sem_out.at[s * per + j]
        )

    def start(s, carry):
        for j in range(per):
            fetch(s, j).start()
        return carry

    def turn(s, carry):
        for j in range(per):
            fetch(s, j).wait()
            ship(s, j).start()
        return carry

    def drain(s, carry):
        for j in range(per):
            ship(s, j).wait()
        return carry

    lax.fori_loop(0, peers, start, 0)
    lax.fori_loop(0, peers, turn, 0)
    lax.fori_loop(0, peers, drain, 0)


def place(table, incoming):
    peers, per = incoming.shape[:2]
    count = peers * per
    return pl.pallas_call(
        place_body,
        out_shape=jax.ShapeDtypeStruct((count,) + incoming.shape[2:], incoming.dtype),
        in_specs=[smem(), hbm()],
        out_specs=hbm(),
        scratch_shapes=[
            pltpu.VMEM((count,) + incoming.shape[2:], incoming.dtype),
            pltpu.SemaphoreType.DMA((count,)),
            pltpu.SemaphoreType.DMA((count,)),
        ],
        compiler_params=pltpu.CompilerParams(vmem_limit_bytes=60 << 20),
        name="place",
    )(table, incoming)


def layer_body(ways, q_heads, kv_heads, *refs):
    (span_ref, lens_ref, table_ref, inv_ref) = refs[:4]
    gains = refs[4 : 4 + ways]
    xs = refs[4 + ways : 4 + 2 * ways]
    wq_ref, wk_ref, wv_ref, wo_ref, cache_ref = refs[4 + 2 * ways : 9 + 2 * ways]
    base_ref = refs[9 + 2 * ways]
    sends = refs[10 + 2 * ways : 9 + 3 * ways]
    (
        x_s, nrm_s, wq_s, wk_s, wv_s, wo_s, kv_s, acc_s, q_s, k_s, v_s, att_s, flat_s,
        cos_s, low_s, high_s, x_sem, w_sem, o_sem, kv_sem,
    ) = refs[9 + 3 * ways :]
    rows, feats = xs[0].shape
    per, reqs = table_ref.shape[1], table_ref.shape[2]
    block_len = cache_ref.shape[-1]
    group = q_heads // kv_heads
    me = lax.axis_index("tp")

    def x_copy(t):
        return pltpu.make_async_copy(xs[t], x_s.at[t], x_sem.at[t])

    w_copies = [
        pltpu.make_async_copy(wq_ref, wq_s, w_sem.at[0]),
        pltpu.make_async_copy(wk_ref, wk_s, w_sem.at[1]),
        pltpu.make_async_copy(wv_ref, wv_s, w_sem.at[2]),
    ]

    def o_copy(t):
        col = pl.multiple_of(lax.rem(me + t, ways) * feats, LANES)
        return pltpu.make_async_copy(wo_ref.at[:, pl.ds(col, feats)], wo_s.at[t], o_sem.at[t])

    def kv_copy(r, j):
        return pltpu.make_async_copy(
            cache_ref.at[table_ref[0, j, r]],
            kv_s.at[r, :, :, pl.ds(0, HEAD_DIM), pl.ds(j * block_len, block_len)],
            kv_sem.at[r * per + j],
        )

    for t in range(ways):
        x_copy(t).start()
    for copy in w_copies:
        copy.start()

    def kv_start(r, carry):
        for j in range(per):
            kv_copy(r, j).start()
        return carry

    lax.fori_loop(0, reqs, kv_start, 0)
    for t in range(ways):
        o_copy(t).start()

    row_id = lax.broadcasted_iota(jnp.int32, (rows, LANES), 0)

    def shift_of(r, carry):
        offset, shift = carry
        shift = jnp.where(row_id >= offset, lens_ref[0, r] - offset, shift)
        return offset + span_ref[0, r], shift

    _, shift = lax.fori_loop(0, reqs, shift_of, (jnp.int32(0), jnp.zeros_like(row_id)))
    angle = (row_id + shift).astype(jnp.float32) * inv_ref[...]
    lane = lax.broadcasted_iota(jnp.int32, (rows, LANES), 1)
    cos_s[...] = jnp.where(lane < HEAD_DIM, jnp.cos(angle), 0.0)
    sine = jnp.sin(angle)
    low_s[...] = jnp.where(lane < HALF, -sine, 0.0)
    high_s[...] = jnp.where((lane >= HALF) & (lane < HEAD_DIM), sine, 0.0)

    pad = kv_s.shape[3] - HEAD_DIM
    zeros_kv = jnp.zeros((2, pad, kv_s.shape[4]), kv_s.dtype)

    def kv_zero(r, carry):
        for g in range(kv_heads):
            kv_s[r, g, :, HEAD_DIM:, :] = zeros_kv
        return carry

    lax.fori_loop(0, reqs, kv_zero, 0)
    acc_s[...] = jnp.zeros(acc_s.shape, acc_s.dtype)
    att_s[...] = jnp.zeros(att_s.shape, att_s.dtype)

    for t in range(ways):
        x_copy(t).wait()
    step = 64

    def norm_rows(m, carry):
        here = pl.ds(pl.multiple_of(m * step, step), step)
        wide = [x_s[t, here, :].astype(jnp.float32) for t in range(ways)]
        total = sum(jnp.sum(w * w, axis=1, keepdims=True) for w in wide)
        scale = lax.rsqrt(total / (ways * feats) + EPS)
        for t in range(ways):
            nrm_s[lax.rem(me + t, ways), here, :] = (
                wide[t] * scale * gains[t][...].astype(jnp.float32)
            ).astype(jnp.bfloat16)
        return carry

    lax.fori_loop(0, rows // step, norm_rows, 0)

    tall = 256

    def project(w_s, first, width, here):
        total = None
        for c in range(ways):
            deep = slice(c * feats, (c + 1) * feats)
            if first is None:
                part = lax.dot_general(
                    nrm_s[c, here, :], w_s[:, deep], NT, preferred_element_type=jnp.float32
                )
            else:
                part = jnp.dot(
                    nrm_s[c, here, :], w_s[deep, first : first + width],
                    preferred_element_type=jnp.float32,
                )
            total = part if total is None else total + part
        acc_s[:, :width] = total

    def head_of(h):
        base = HEAD_DIM * h // LANES * LANES
        shift = HEAD_DIM * h - base
        wide = acc_s[:, base : base + 2 * LANES]
        if shift:
            wide = pltpu.roll(wide, 2 * LANES - shift, 1)
        return wide[:, :LANES]

    def rotated(h, here):
        value = head_of(h)
        return (
            value * cos_s[here, :]
            + pltpu.roll(value, LANES - HALF, 1) * low_s[here, :]
            + pltpu.roll(value, HALF, 1) * high_s[here, :]
        ).astype(jnp.bfloat16)

    for copy in w_copies:
        copy.wait()
    block_heads = min(8, q_heads)

    def project_rows(m, carry):
        here = pl.ds(pl.multiple_of(m * tall, tall), tall)
        project(wk_s, None, kv_heads * HEAD_DIM, here)
        for g in range(kv_heads):
            k_s[g, here, :] = rotated(g, here)
        project(wv_s, None, kv_heads * HEAD_DIM, here)
        narrow = lax.broadcasted_iota(jnp.int32, (tall, LANES), 1) < HEAD_DIM
        for g in range(kv_heads):
            v_s[g, here, :] = jnp.where(narrow, head_of(g), 0.0).astype(jnp.bfloat16)
        for block in range(q_heads // block_heads):
            project(wq_s, block * block_heads * HEAD_DIM, block_heads * HEAD_DIM, here)
            for h in range(block_heads):
                q_s[block * block_heads + h, here, :] = rotated(h, here)
        return carry

    lax.fori_loop(0, rows // tall, project_rows, 0)

    log_scale = (1.0 / math.sqrt(HEAD_DIM)) * math.log2(math.e)
    keys_old = per * block_len

    def request(r, offset):
        span = span_ref[0, r]
        prior = lens_ref[0, r]
        for j in range(per):
            kv_copy(r, j).wait()
        first = offset // 16 * 16
        key_first = pl.multiple_of(jnp.minimum(first, rows - LANES), 16)
        old_ok = lax.broadcasted_iota(jnp.int32, (1, keys_old), 1) < prior

        def tile(i, carry):
            begin = pl.multiple_of(first + i * ROWS, 16)
            here = pl.ds(begin, ROWS)
            row = begin + lax.broadcasted_iota(jnp.int32, (ROWS, LANES), 0)
            key = key_first + lax.broadcasted_iota(jnp.int32, (ROWS, LANES), 1)
            new_ok = ((key <= row) & (key >= offset))[None]
            keep = ((row >= offset) & (row < offset + span))[None]
            for g in range(kv_heads):
                heads = slice(g * group, (g + 1) * group)
                query = q_s[heads, here, :].reshape(group * ROWS, LANES)
                old = jnp.dot(query, kv_s[r, g, 0], preferred_element_type=jnp.float32)
                new = lax.dot_general(
                    query, k_s[g, pl.ds(key_first, LANES), :], NT,
                    preferred_element_type=jnp.float32,
                )
                old = jnp.where(old_ok, old, MASKED)
                new = jnp.where(new_ok, new.reshape(group, ROWS, LANES), MASKED)
                new = new.reshape(group * ROWS, LANES)
                top = jnp.maximum(
                    jnp.max(old, axis=1, keepdims=True), jnp.max(new, axis=1, keepdims=True)
                )
                old = jnp.exp2((old - top) * log_scale)
                new = jnp.exp2((new - top) * log_scale)
                total = jnp.sum(old, axis=1, keepdims=True) + jnp.sum(new, axis=1, keepdims=True)
                mixed = lax.dot_general(
                    old.astype(jnp.bfloat16), kv_s[r, g, 1], NT,
                    preferred_element_type=jnp.float32,
                ) + jnp.dot(
                    new.astype(jnp.bfloat16), v_s[g, pl.ds(key_first, LANES), :],
                    preferred_element_type=jnp.float32,
                )
                mixed = (mixed / total).reshape(group, ROWS, LANES)
                att_s[heads, here, :] = jnp.where(keep, mixed, att_s[heads, here, :])
            return carry

        lax.fori_loop(0, (offset - first + span + ROWS - 1) // ROWS, tile, 0)
        return offset + span

    lax.fori_loop(0, reqs, request, jnp.int32(0))

    for t in range(ways):
        o_copy(t).wait()

    def out_rows(m, carry):
        here = pl.ds(pl.multiple_of(m * tall, tall), tall)
        flat_s[...] = jnp.zeros(flat_s.shape, flat_s.dtype)
        for h in range(q_heads):
            base = HEAD_DIM * h // LANES * LANES
            shift = HEAD_DIM * h - base
            value = att_s[h, here, :]
            wide = jnp.concatenate([value, jnp.zeros_like(value)], axis=1)
            if shift:
                wide = pltpu.roll(wide, shift, 1)
            flat_s[:, base : base + 2 * LANES] += wide
        flat = flat_s[:, : q_heads * HEAD_DIM].astype(jnp.bfloat16)
        for t in range(ways):
            part = jnp.dot(flat, wo_s[t], preferred_element_type=jnp.float32)
            if t == 0:
                base_ref[here, :] = x_s[0, here, :].astype(jnp.float32) + part
            else:
                sends[t - 1][here, :] = part.astype(jnp.bfloat16)
        return carry

    lax.fori_loop(0, rows // tall, out_rows, 0)


def layer(ways, spans, lens, table, gains, xs, w_query, w_key, w_value, w_out, cache):
    rows, feats = xs[0].shape
    q_heads = w_query.shape[1] // HEAD_DIM
    kv_heads = w_key.shape[0] // HEAD_DIM
    per, reqs = table.shape[1], table.shape[2]
    keys = per * cache.shape[-1]
    pairs = np.arange(LANES) % HALF
    inverse = np.where(
        np.arange(LANES) < HEAD_DIM, np.float64(THETA) ** (-2.0 * pairs / HEAD_DIM), 0.0
    ).astype(np.float32)[None]
    bf, f32 = jnp.bfloat16, jnp.float32
    outs = pl.pallas_call(
        functools.partial(layer_body, ways, q_heads, kv_heads),
        out_shape=[jax.ShapeDtypeStruct((rows, feats), f32)]
        + [jax.ShapeDtypeStruct((rows, feats), bf)] * (ways - 1),
        in_specs=[smem(), smem(), smem(), vmem()] + [vmem()] * ways + [hbm()] * (ways + 5),
        out_specs=[vmem()] * ways,
        scratch_shapes=[
            pltpu.VMEM((ways, rows, feats), bf),
            pltpu.VMEM((ways, rows, feats), bf),
            pltpu.VMEM(w_query.shape, bf),
            pltpu.VMEM(w_key.shape, bf),
            pltpu.VMEM(w_value.shape, bf),
            pltpu.VMEM((ways, w_out.shape[0], feats), bf),
            pltpu.VMEM((reqs, kv_heads, 2, LANES, keys), bf),
            pltpu.VMEM((256, min(8, q_heads) * HEAD_DIM + LANES), f32),
            pltpu.VMEM((q_heads, rows + ROWS, LANES), bf),
            pltpu.VMEM((kv_heads, rows, LANES), bf),
            pltpu.VMEM((kv_heads, rows, LANES), bf),
            pltpu.VMEM((q_heads, rows + ROWS, LANES), f32),
            pltpu.VMEM((256, q_heads * HEAD_DIM + LANES), f32),
            pltpu.VMEM((rows, LANES), f32),
            pltpu.VMEM((rows, LANES), f32),
            pltpu.VMEM((rows, LANES), f32),
            pltpu.SemaphoreType.DMA((ways,)),
            pltpu.SemaphoreType.DMA((3,)),
            pltpu.SemaphoreType.DMA((ways,)),
            pltpu.SemaphoreType.DMA((reqs * per,)),
        ],
        compiler_params=pltpu.CompilerParams(vmem_limit_bytes=60 << 20),
        cost_estimate=pl.CostEstimate(
            flops=100 * 2 * rows * ways * feats * 2 * w_query.shape[1],
            transcendentals=0,
            bytes_accessed=4 * w_query.size,
        ),
        name="layer",
    )(spans, lens, table, jnp.asarray(inverse), *gains, *xs, w_query, w_key, w_value, w_out, cache)
    return outs[0], outs[1:]


def local(
    tokens,
    norm_gain,
    w_query,
    w_key,
    w_value,
    w_out,
    prior_cache,
    prior_lens,
    span_lens,
    prior_table,
    dest_device,
    dest_table,
):
    ways = lax.axis_size("tp")
    gain = norm_gain[None, :]
    w_key, w_value = w_key.T, w_value.T
    prior_table = prior_table.transpose(0, 2, 1)
    dest_table = dest_table.transpose(0, 2, 1)

    def from_peer(value, t):
        return lax.ppermute(value, "tp", [((d + t) % ways, d) for d in range(ways)])

    def to_peer(value, t):
        return lax.ppermute(value, "tp", [(d, (d + t) % ways) for d in range(ways)])

    outgoing = pack(dest_device, prior_lens, prior_table, prior_cache)
    incoming = lax.all_to_all(outgoing, "seq", split_axis=0, concat_axis=0, tiled=True)
    xs = [tokens] + [from_peer(tokens, t) for t in range(1, ways)]
    gains = [gain] + [from_peer(gain, t) for t in range(1, ways)]
    base, sends = layer(
        ways, span_lens, prior_lens, prior_table, gains, xs,
        w_query, w_key, w_value, w_out, prior_cache,
    )
    total = base
    for t in range(1, ways):
        total = total + to_peer(sends[t - 1], t).astype(jnp.float32)
    hidden = total.astype(jnp.bfloat16)
    decode_cache = place(dest_table, incoming)
    return (hidden, decode_cache)


def solution(mesh):
    in_specs = (
        P("seq", "tp"),
        P("tp"),
        P(None, "tp"),
        P(None, "tp"),
        P(None, "tp"),
        P("tp", None),
        P("seq", "tp", None, None, None),
        P("seq", None),
        P("seq", None),
        P("seq", None, None),
        P("seq", None),
        P("seq", None, None),
    )
    out_specs = (P("seq", "tp"), P("seq", "tp", None, None, None))
    return jax.shard_map(local, mesh=mesh, in_specs=in_specs, out_specs=out_specs, check_vma=False)
```

```python
import functools
import math

import jax
import jax.numpy as jnp
import numpy as np
from jax import lax
from jax.experimental import pallas as pl
from jax.experimental.pallas import tpu as pltpu
from jax.sharding import PartitionSpec as P

HEAD_DIM = 80
HALF = HEAD_DIM // 2
LANES = 128
WINDOW = 64
EPS = 1e-05
THETA = 1000000.0
MASKED = -1e30
ROWS = 64
SIDE_VMEM = 62 << 20
LAYER_VMEM = 62 << 20
NT = (((1,), (1,)), ((), ()))


def smem():
    return pl.BlockSpec(memory_space=pltpu.SMEM)


def vmem():
    return pl.BlockSpec(memory_space=pltpu.VMEM)


def hbm():
    return pl.BlockSpec(memory_space=pl.ANY)


def pack_body(hops, dest_ref, lens_ref, table_ref, cache_ref, *refs):
    outs = refs[: len(hops)]
    inverse, buf, sem_in, sem_out = refs[-4:]
    reqs = dest_ref.shape[1]
    per = table_ref.shape[1]
    block_len = cache_ref.shape[-1]
    me = lax.axis_index("seq")

    def invert(r, carry):
        inverse[dest_ref[0, r]] = r
        return carry

    lax.fori_loop(0, reqs, invert, 0)
    steps = []
    for ref, group in zip(outs, hops):
        for e, hop in enumerate(group):
            for j in range(per):
                steps.append((len(steps), ref, e, hop, j))

    def count_of(hop, j):
        return lens_ref[0, inverse[jnp.bitwise_xor(me, hop)]] - j * block_len

    def fetch(i, hop, j):
        row = table_ref[0, j, inverse[jnp.bitwise_xor(me, hop)]]
        return pltpu.make_async_copy(cache_ref.at[row], buf.at[i], sem_in.at[i])

    def ship(i, ref, e, j):
        return pltpu.make_async_copy(buf.at[i], ref.at[e, j], sem_out.at[i])

    for i, ref, e, hop, j in steps:
        @pl.when(count_of(hop, j) > 0)
        def _():
            fetch(i, hop, j).start()

    for i, ref, e, hop, j in steps:
        count = count_of(hop, j)

        @pl.when(count > 0)
        def _():
            fetch(i, hop, j).wait()

        @pl.when(count < block_len)
        def _():
            block = buf[i]
            lane = lax.broadcasted_iota(jnp.int32, block.shape, block.ndim - 1)
            buf[i] = jnp.where(lane < count, block.astype(jnp.float32), 0.0).astype(jnp.bfloat16)

        ship(i, ref, e, j).start()

    for i, ref, e, hop, j in steps:
        ship(i, ref, e, j).wait()


def pack(hops, dest, lens, table, cache, after):
    per, reqs = table.shape[1], table.shape[2]
    count = sum(len(group) for group in hops) * per
    tail = cache.shape[1:]

    def body(*refs):
        pack_body(hops, *refs[:4], *refs[4 + len(after) :])

    return pl.pallas_call(
        body,
        out_shape=[jax.ShapeDtypeStruct((len(group), per) + tail, cache.dtype) for group in hops],
        in_specs=[smem(), smem(), smem(), hbm()] + [hbm()] * len(after),
        out_specs=[hbm()] * len(hops),
        scratch_shapes=[
            pltpu.SMEM((reqs,), jnp.int32),
            pltpu.VMEM((count,) + tail, cache.dtype),
            pltpu.SemaphoreType.DMA((count,)),
            pltpu.SemaphoreType.DMA((count,)),
        ],
        compiler_params=pltpu.CompilerParams(vmem_limit_bytes=SIDE_VMEM),
        name="pack",
    )(dest, lens, table, cache, *after)


def relay_body(*refs):
    out_ref, buf, sem_in, sem_out = refs[-4:]
    ins = refs[: out_ref.shape[0]]
    for i, ref in enumerate(ins):
        pltpu.make_async_copy(ref.at[ref.shape[0] - 1], buf.at[i], sem_in.at[i]).start()
    for i, ref in enumerate(ins):
        pltpu.make_async_copy(ref.at[ref.shape[0] - 1], buf.at[i], sem_in.at[i]).wait()
        pltpu.make_async_copy(buf.at[i], out_ref.at[i], sem_out.at[i]).start()
    for i, ref in enumerate(ins):
        pltpu.make_async_copy(buf.at[i], out_ref.at[i], sem_out.at[i]).wait()


def relay(arrays, after):
    shape = (len(arrays),) + arrays[0].shape[1:]
    return pl.pallas_call(
        relay_body,
        out_shape=jax.ShapeDtypeStruct(shape, arrays[0].dtype),
        in_specs=[hbm()] * (len(arrays) + len(after)),
        out_specs=hbm(),
        scratch_shapes=[
            pltpu.VMEM(shape, arrays[0].dtype),
            pltpu.SemaphoreType.DMA((len(arrays),)),
            pltpu.SemaphoreType.DMA((len(arrays),)),
        ],
        compiler_params=pltpu.CompilerParams(vmem_limit_bytes=SIDE_VMEM),
        name="relay",
    )(*arrays, *after)


def place(table, arrays, sources, rows):
    per = table.shape[1]
    count = len(sources) * per
    tail = arrays[0].shape[2:]
    moves = [(which, e, hop, j) for which, e, hop in sources for j in range(per)]

    def body(table_ref, *refs):
        ins = refs[: len(arrays)]
        out_ref, buf, sem_in, sem_out = refs[-4:]
        me = lax.axis_index("seq")

        def fetch(i, which, e, j):
            return pltpu.make_async_copy(ins[which].at[e, j], buf.at[i], sem_in.at[i])

        def ship(i, hop, j):
            row = table_ref[0, j, jnp.bitwise_xor(me, hop)]
            return pltpu.make_async_copy(buf.at[i], out_ref.at[row], sem_out.at[i])

        for i, (which, e, hop, j) in enumerate(moves):
            fetch(i, which, e, j).start()
        for i, (which, e, hop, j) in enumerate(moves):
            fetch(i, which, e, j).wait()
            ship(i, hop, j).start()
        for i, (which, e, hop, j) in enumerate(moves):
            ship(i, hop, j).wait()

    return pl.pallas_call(
        body,
        out_shape=jax.ShapeDtypeStruct((rows,) + tail, arrays[0].dtype),
        in_specs=[smem()] + [hbm()] * len(arrays),
        out_specs=hbm(),
        scratch_shapes=[
            pltpu.VMEM((count,) + tail, arrays[0].dtype),
            pltpu.SemaphoreType.DMA((count,)),
            pltpu.SemaphoreType.DMA((count,)),
        ],
        compiler_params=pltpu.CompilerParams(vmem_limit_bytes=SIDE_VMEM),
        name="place",
    )(table, *arrays)


def place_last(table, arrays, hops, made):
    per = table.shape[1]
    moves = [(which, hop, j) for which, hop in enumerate(hops) for j in range(per)]

    def body(table_ref, *refs):
        out_ref, sem = refs[-2:]
        me = lax.axis_index("seq")

        def ship(i, which, hop, j):
            row = table_ref[0, j, jnp.bitwise_xor(me, hop)]
            return pltpu.make_async_copy(refs[which].at[0, j], out_ref.at[row], sem.at[i])

        for i, move in enumerate(moves):
            ship(i, *move).start()
        for i, move in enumerate(moves):
            ship(i, *move).wait()

    return pl.pallas_call(
        body,
        out_shape=jax.ShapeDtypeStruct(made.shape, made.dtype),
        in_specs=[smem()] + [vmem()] * len(arrays) + [hbm()],
        out_specs=hbm(),
        scratch_shapes=[pltpu.SemaphoreType.DMA((len(moves),))],
        input_output_aliases={1 + len(arrays): 0},
        compiler_params=pltpu.CompilerParams(vmem_limit_bytes=4 << 20),
        name="place_last",
    )(table, *arrays, made)


def layer_body(ways, q_heads, kv_heads, *refs):
    (span_ref, lens_ref, table_ref, inv_ref) = refs[:4]
    gains = refs[4 : 4 + ways]
    xs = refs[4 + ways : 4 + 2 * ways]
    wq_ref, wk_ref, wv_ref, wo_ref, cache_ref = refs[4 + 2 * ways : 9 + 2 * ways]
    base_ref = refs[9 + 2 * ways]
    sends = refs[10 + 2 * ways : 9 + 3 * ways]
    (
        x_s, nrm_s, wq_s, wk_s, wv_s, wo_s, kv_s, acc_s, q_s, k_s, v_s, att_s, flat_s,
        cos_s, low_s, high_s, x_sem, w_sem, o_sem, kv_sem,
    ) = refs[9 + 3 * ways :]
    rows, feats = xs[0].shape
    per, reqs = table_ref.shape[1], table_ref.shape[2]
    block_len = cache_ref.shape[-1]
    group = q_heads // kv_heads
    me = lax.axis_index("tp")

    def x_copy(t):
        return pltpu.make_async_copy(xs[t], x_s.at[t], x_sem.at[t])

    w_copies = [
        pltpu.make_async_copy(wq_ref, wq_s, w_sem.at[0]),
        pltpu.make_async_copy(wk_ref, wk_s, w_sem.at[1]),
        pltpu.make_async_copy(wv_ref, wv_s, w_sem.at[2]),
    ]

    def o_copy(t):
        col = pl.multiple_of(lax.rem(me + t, ways) * feats, LANES)
        return pltpu.make_async_copy(wo_ref.at[:, pl.ds(col, feats)], wo_s.at[t], o_sem.at[t])

    def kv_copy(r, j):
        return pltpu.make_async_copy(
            cache_ref.at[table_ref[0, j, r]],
            kv_s.at[r, :, :, pl.ds(0, HEAD_DIM), pl.ds(j * block_len, block_len)],
            kv_sem.at[r * per + j],
        )

    for t in range(ways):
        x_copy(t).start()
    for copy in w_copies:
        copy.start()

    def kv_start(r, carry):
        for j in range(per):
            kv_copy(r, j).start()
        return carry

    lax.fori_loop(0, reqs, kv_start, 0)
    for t in range(ways):
        o_copy(t).start()

    row_id = lax.broadcasted_iota(jnp.int32, (rows, LANES), 0)

    def shift_of(r, carry):
        offset, shift = carry
        shift = jnp.where(row_id >= offset, lens_ref[0, r] - offset, shift)
        return offset + span_ref[0, r], shift

    _, shift = lax.fori_loop(0, reqs, shift_of, (jnp.int32(0), jnp.zeros_like(row_id)))
    angle = (row_id + shift).astype(jnp.float32) * inv_ref[...]
    lane = lax.broadcasted_iota(jnp.int32, (rows, LANES), 1)
    cos_s[...] = jnp.where(lane < HEAD_DIM, jnp.cos(angle), 0.0)
    sine = jnp.sin(angle)
    low_s[...] = jnp.where(lane < HALF, -sine, 0.0)
    high_s[...] = jnp.where((lane >= HALF) & (lane < HEAD_DIM), sine, 0.0)

    pad = kv_s.shape[3] - HEAD_DIM
    zeros_kv = jnp.zeros((2, pad, kv_s.shape[4]), kv_s.dtype)

    def kv_zero(r, carry):
        for g in range(kv_heads):
            kv_s[r, g, :, HEAD_DIM:, :] = zeros_kv
        return carry

    lax.fori_loop(0, reqs, kv_zero, 0)
    acc_s[...] = jnp.zeros(acc_s.shape, acc_s.dtype)

    for t in range(ways):
        x_copy(t).wait()
    step = 64

    def norm_rows(m, carry):
        here = pl.ds(pl.multiple_of(m * step, step), step)
        wide = [x_s[t, here, :].astype(jnp.float32) for t in range(ways)]
        total = sum(jnp.sum(w * w, axis=1, keepdims=True) for w in wide)
        scale = lax.rsqrt(total / (ways * feats) + EPS)
        for t in range(ways):
            nrm_s[lax.rem(me + t, ways), here, :] = (
                wide[t] * scale * gains[t][...].astype(jnp.float32)
            ).astype(jnp.bfloat16)
        return carry

    lax.fori_loop(0, rows // step, norm_rows, 0)

    tall = 256

    def project(w_s, first, width, here):
        total = None
        for c in range(ways):
            deep = slice(c * feats, (c + 1) * feats)
            if first is None:
                part = lax.dot_general(
                    nrm_s[c, here, :], w_s[:, deep], NT, preferred_element_type=jnp.float32
                )
            else:
                part = jnp.dot(
                    nrm_s[c, here, :], w_s[deep, first : first + width],
                    preferred_element_type=jnp.float32,
                )
            total = part if total is None else total + part
        acc_s[:, :width] = total

    def head_of(h):
        base = HEAD_DIM * h // LANES * LANES
        shift = HEAD_DIM * h - base
        wide = acc_s[:, base : base + 2 * LANES]
        if shift:
            wide = pltpu.roll(wide, 2 * LANES - shift, 1)
        return wide[:, :LANES]

    def rotated(h, here):
        value = head_of(h)
        return (
            value * cos_s[here, :]
            + pltpu.roll(value, LANES - HALF, 1) * low_s[here, :]
            + pltpu.roll(value, HALF, 1) * high_s[here, :]
        ).astype(jnp.bfloat16)

    for copy in w_copies:
        copy.wait()
    block_heads = min(8, q_heads)

    def project_rows(m, carry):
        here = pl.ds(pl.multiple_of(m * tall, tall), tall)
        project(wk_s, None, kv_heads * HEAD_DIM, here)
        for g in range(kv_heads):
            k_s[g, here, :] = rotated(g, here)
        project(wv_s, None, kv_heads * HEAD_DIM, here)
        narrow = lax.broadcasted_iota(jnp.int32, (tall, LANES), 1) < HEAD_DIM
        for g in range(kv_heads):
            v_s[g, here, :] = jnp.where(narrow, head_of(g), 0.0).astype(jnp.bfloat16)
        for block in range(q_heads // block_heads):
            project(wq_s, block * block_heads * HEAD_DIM, block_heads * HEAD_DIM, here)
            for h in range(block_heads):
                q_s[block * block_heads + h, here, :] = rotated(h, here)
        return carry

    lax.fori_loop(0, rows // tall, project_rows, 0)

    log_scale = (1.0 / math.sqrt(HEAD_DIM)) * math.log2(math.e)
    keys_old = per * block_len

    def request(r, offset):
        span = span_ref[0, r]
        prior = lens_ref[0, r]
        for j in range(per):
            kv_copy(r, j).wait()
        first = offset // 16 * 16
        key_first = pl.multiple_of(jnp.minimum(first, rows - LANES), 16)
        old_ok = lax.broadcasted_iota(jnp.int32, (1, keys_old), 1) < prior

        def tile(i, carry):
            begin = pl.multiple_of(first + i * ROWS, 16)
            here = pl.ds(begin, ROWS)
            row = begin + lax.broadcasted_iota(jnp.int32, (ROWS, LANES), 0)
            key = key_first + lax.broadcasted_iota(jnp.int32, (ROWS, LANES), 1)
            new_ok = ((key <= row) & (key >= offset))[None]
            keep = ((row >= offset) & (row < offset + span))[None]
            scores = []
            for g in range(kv_heads):
                heads = slice(g * group, (g + 1) * group)
                query = q_s[heads, here, :].reshape(group * ROWS, LANES)
                old = jnp.dot(query, kv_s[r, g, 0], preferred_element_type=jnp.float32)
                new = lax.dot_general(
                    query, k_s[g, pl.ds(key_first, LANES), :], NT,
                    preferred_element_type=jnp.float32,
                )
                scores.append((old, new))
            probs = []
            for old, new in scores:
                old = jnp.where(old_ok, old, MASKED)
                new = jnp.where(new_ok, new.reshape(group, ROWS, LANES), MASKED)
                new = new.reshape(group * ROWS, LANES)
                wide = jnp.maximum(jnp.maximum(old[:, :LANES], old[:, LANES:]), new)
                top = jnp.max(wide, axis=1, keepdims=True)
                old = jnp.exp2((old - top) * log_scale)
                new = jnp.exp2((new - top) * log_scale)
                wide = old[:, :LANES] + old[:, LANES:] + new
                total = jnp.sum(wide, axis=1, keepdims=True)
                probs.append((old.astype(jnp.bfloat16), new.astype(jnp.bfloat16), total))
            for g in range(kv_heads):
                heads = slice(g * group, (g + 1) * group)
                old, new, total = probs[g]
                mixed = lax.dot_general(
                    old, kv_s[r, g, 1], NT, preferred_element_type=jnp.float32,
                ) + jnp.dot(
                    new, v_s[g, pl.ds(key_first, LANES), :],
                    preferred_element_type=jnp.float32,
                )
                mixed = (mixed / total).reshape(group, ROWS, LANES)
                att_s[heads, here, :] = jnp.where(keep, mixed, att_s[heads, here, :])
            return carry

        lax.fori_loop(0, (offset - first + span + ROWS - 1) // ROWS, tile, 0)
        return offset + span

    lax.fori_loop(0, reqs, request, jnp.int32(0))

    for t in range(ways):
        o_copy(t).wait()

    def out_rows(m, carry):
        here = pl.ds(pl.multiple_of(m * tall, tall), tall)
        flat_s[...] = jnp.zeros(flat_s.shape, flat_s.dtype)
        for h in range(q_heads):
            base = HEAD_DIM * h // LANES * LANES
            shift = HEAD_DIM * h - base
            value = att_s[h, here, :]
            wide = jnp.concatenate([value, jnp.zeros_like(value)], axis=1)
            if shift:
                wide = pltpu.roll(wide, shift, 1)
            flat_s[:, base : base + 2 * LANES] += wide
        flat = flat_s[:, : q_heads * HEAD_DIM].astype(jnp.bfloat16)
        for t in range(ways):
            part = jnp.dot(flat, wo_s[t], preferred_element_type=jnp.float32)
            if t == 0:
                base_ref[here, :] = x_s[0, here, :].astype(jnp.float32) + part
            else:
                sends[t - 1][here, :] = part.astype(jnp.bfloat16)
        return carry

    lax.fori_loop(0, rows // tall, out_rows, 0)


def layer(ways, spans, lens, table, gains, xs, w_query, w_key, w_value, w_out, cache):
    rows, feats = xs[0].shape
    q_heads = w_query.shape[1] // HEAD_DIM
    kv_heads = w_key.shape[0] // HEAD_DIM
    per, reqs = table.shape[1], table.shape[2]
    keys = per * cache.shape[-1]
    pairs = np.arange(LANES) % HALF
    inverse = np.where(
        np.arange(LANES) < HEAD_DIM, np.float64(THETA) ** (-2.0 * pairs / HEAD_DIM), 0.0
    ).astype(np.float32)[None]
    bf, f32 = jnp.bfloat16, jnp.float32
    outs = pl.pallas_call(
        functools.partial(layer_body, ways, q_heads, kv_heads),
        out_shape=[jax.ShapeDtypeStruct((rows, feats), f32)]
        + [jax.ShapeDtypeStruct((rows, feats), bf)] * (ways - 1),
        in_specs=[smem(), smem(), smem(), vmem()] + [vmem()] * ways + [hbm()] * (ways + 5),
        out_specs=[vmem()] * ways,
        scratch_shapes=[
            pltpu.VMEM((ways, rows, feats), bf),
            pltpu.VMEM((ways, rows, feats), bf),
            pltpu.VMEM(w_query.shape, bf),
            pltpu.VMEM(w_key.shape, bf),
            pltpu.VMEM(w_value.shape, bf),
            pltpu.VMEM((ways, w_out.shape[0], feats), bf),
            pltpu.VMEM((reqs, kv_heads, 2, LANES, keys), bf),
            pltpu.VMEM((256, min(8, q_heads) * HEAD_DIM + LANES), f32),
            pltpu.VMEM((q_heads, rows + ROWS, LANES), bf),
            pltpu.VMEM((kv_heads, rows, LANES), bf),
            pltpu.VMEM((kv_heads, rows, LANES), bf),
            pltpu.VMEM((q_heads, rows + ROWS, LANES), f32),
            pltpu.VMEM((256, q_heads * HEAD_DIM + LANES), f32),
            pltpu.VMEM((rows, LANES), f32),
            pltpu.VMEM((rows, LANES), f32),
            pltpu.VMEM((rows, LANES), f32),
            pltpu.SemaphoreType.DMA((ways,)),
            pltpu.SemaphoreType.DMA((3,)),
            pltpu.SemaphoreType.DMA((ways,)),
            pltpu.SemaphoreType.DMA((reqs * per,)),
        ],
        compiler_params=pltpu.CompilerParams(vmem_limit_bytes=LAYER_VMEM),
        cost_estimate=pl.CostEstimate(
            flops=100 * 2 * rows * ways * feats * 2 * w_query.shape[1],
            transcendentals=0,
            bytes_accessed=4 * w_query.size,
        ),
        name="layer",
    )(spans, lens, table, jnp.asarray(inverse), *gains, *xs, w_query, w_key, w_value, w_out, cache)
    return outs[0], outs[1:]


def local(
    tokens,
    norm_gain,
    w_query,
    w_key,
    w_value,
    w_out,
    prior_cache,
    prior_lens,
    span_lens,
    prior_table,
    dest_device,
    dest_table,
):
    ways = lax.axis_size("tp")
    w_key, w_value = w_key.T, w_value.T
    prior_table = prior_table.transpose(0, 2, 1)
    dest_table = dest_table.transpose(0, 2, 1)
    def from_peer(value, t):
        return lax.ppermute(value, "tp", [((d + t) % ways, d) for d in range(ways)])

    def to_peer(value, t):
        return lax.ppermute(value, "tp", [(d, (d + t) % ways) for d in range(ways)])

    peers = lax.axis_size("seq")
    pairs = peers // 2

    def to_hop(value, hop):
        return lax.ppermute(value, "seq", [(d, d ^ hop) for d in range(peers)])

    barrier = lax.optimization_barrier
    far = list(range(pairs // 2, pairs))
    near = list(range(1, pairs // 2))
    args = (dest_device, prior_lens, prior_table, prior_cache)
    begin = [far[0]] + near[:-1]
    middle = far[1:-2] + near[-1:]
    direct = [2 * far[-1]]
    late = [2 * far[-2], 2 * far[-2] + 1, 2 * far[-1] + 1]
    pair = lambda k: (2 * k, 2 * k + 1)
    xs = [tokens] + [from_peer(tokens, t) for t in range(1, ways)]
    begin_out = pack([pair(begin[0])], *args, [])
    begin_out += pack([pair(k) for k in begin[1:]], *args, begin_out)
    begin_in = [to_hop(value, 2 * k) for k, value in zip(begin, begin_out)]
    hops = [pair(k) for k in middle] + [(hop,) for hop in direct + late] + [(0, 1)]
    rest = pack(hops, *args, begin_out[-1:])
    own = rest[-1]
    gain = barrier((norm_gain, own))[0][None, :]
    gains = [gain] + [from_peer(gain, t) for t in range(1, ways)]

    ended = begin_in[:1] + [xs[-1]] + begin_in[1:]
    middle_in = []
    for i, value in enumerate(rest[: len(middle) + 1]):
        value = barrier((value, ended[i % len(ended)]))[0]
        middle_in.append(to_hop(value, hops[i][0]))
    xs, begin_in = barrier((xs, begin_in))
    base, sends = layer(
        ways, span_lens, prior_lens, prior_table, gains, xs,
        w_query, w_key, w_value, w_out, prior_cache,
    )
    sends, middle_in, late_out = barrier((sends, middle_in, rest[len(middle) + 1 : -1]))
    late_in = [to_hop(value, hop) for hop, value in zip(late, late_out)]
    total = base
    for t in range(1, ways):
        total = total + to_peer(sends[t - 1], t).astype(jnp.float32)
    hidden = total.astype(jnp.bfloat16)

    arrived = begin_in + middle_in[:-1]
    other = to_hop(relay(arrived + [own], [base]), 1)
    rows = prior_cache.shape[0]
    reach = [2 * k for k in begin + middle] + [0]
    sources = [(i, 0, hop) for i, hop in enumerate(reach)]
    sources += [(len(reach), i, hop + 1) for i, hop in enumerate(reach)]
    sources += [(len(reach) + 1, 0, direct[0])]
    made = place(dest_table, arrived + [own, other, middle_in[-1]], sources, rows)
    decode_cache = place_last(dest_table, late_in, late, made)
    return (hidden, decode_cache)


def solution(mesh):
    in_specs = (
        P("seq", "tp"),
        P("tp"),
        P(None, "tp"),
        P(None, "tp"),
        P(None, "tp"),
        P("tp", None),
        P("seq", "tp", None, None, None),
        P("seq", None),
        P("seq", None),
        P("seq", None, None),
        P("seq", None),
        P("seq", None, None),
    )
    out_specs = (P("seq", "tp"), P("seq", "tp", None, None, None))
    return jax.shard_map(local, mesh=mesh, in_specs=in_specs, out_specs=out_specs, check_vma=False)
```

```python
import functools
import math

import jax
import jax.numpy as jnp
import numpy as np
from jax import lax
from jax.experimental import pallas as pl
from jax.experimental.pallas import tpu as pltpu
from jax.sharding import PartitionSpec as P

HEAD_DIM = 80
HALF = HEAD_DIM // 2
LANES = 128
WINDOW = 64
EPS = 1e-05
THETA = 1000000.0
MASKED = -1e30
ROWS = 64
BY_PERMUTE = 1
SIDE_VMEM = 62 << 20
LAYER_VMEM = 62 << 20
NT = (((1,), (1,)), ((), ()))


def smem():
    return pl.BlockSpec(memory_space=pltpu.SMEM)


def vmem():
    return pl.BlockSpec(memory_space=pltpu.VMEM)


def hbm():
    return pl.BlockSpec(memory_space=pl.ANY)


def pack_body(hops, first, absolute, dest_ref, lens_ref, table_ref, cache_ref, *refs):
    outs = refs[: len(hops)]
    inverse, buf, sem_in, sem_out = refs[-4:]
    reqs = dest_ref.shape[1]
    per = table_ref.shape[1]
    block_len = cache_ref.shape[-1]
    me = 0 if absolute else lax.axis_index("seq")
    heads = outs[0].shape[2]

    def invert(r, carry):
        inverse[dest_ref[0, r]] = r
        return carry

    lax.fori_loop(0, reqs, invert, 0)
    steps = []
    for ref, group in zip(outs, hops):
        for e, hop in enumerate(group):
            for j in range(per):
                steps.append((len(steps), ref, e, hop, j))

    def toward(hop):
        return hop if absolute else jnp.bitwise_xor(me, hop)

    def count_of(hop, j):
        return lens_ref[0, inverse[toward(hop)]] - j * block_len

    def fetch(i, hop, j):
        row = table_ref[0, j, inverse[toward(hop)]]
        return pltpu.make_async_copy(
            cache_ref.at[row, pl.ds(first, heads)], buf.at[i], sem_in.at[i]
        )

    def ship(i, ref, e, j):
        return pltpu.make_async_copy(buf.at[i], ref.at[e, j], sem_out.at[i])

    for i, ref, e, hop, j in steps:
        @pl.when(count_of(hop, j) > 0)
        def _():
            fetch(i, hop, j).start()

    for i, ref, e, hop, j in steps:
        count = count_of(hop, j)

        @pl.when(count > 0)
        def _():
            fetch(i, hop, j).wait()

        @pl.when(count < block_len)
        def _():
            block = buf[i]
            lane = lax.broadcasted_iota(jnp.int32, block.shape, block.ndim - 1)
            buf[i] = jnp.where(lane < count, block.astype(jnp.float32), 0.0).astype(jnp.bfloat16)

        ship(i, ref, e, j).start()

    for i, ref, e, hop, j in steps:
        ship(i, ref, e, j).wait()


def pack(hops, dest, lens, table, cache, after, first, heads, absolute=False):
    per, reqs = table.shape[1], table.shape[2]
    count = sum(len(group) for group in hops) * per
    tail = (heads,) + cache.shape[2:]

    def body(*refs):
        pack_body(hops, first, absolute, *refs[:4], *refs[4 + len(after) :])

    return pl.pallas_call(
        body,
        out_shape=[jax.ShapeDtypeStruct((len(group), per) + tail, cache.dtype) for group in hops],
        in_specs=[smem(), smem(), smem(), hbm()] + [hbm()] * len(after),
        out_specs=[hbm()] * len(hops),
        scratch_shapes=[
            pltpu.SMEM((reqs,), jnp.int32),
            pltpu.VMEM((count,) + tail, cache.dtype),
            pltpu.SemaphoreType.DMA((count,)),
            pltpu.SemaphoreType.DMA((count,)),
        ],
        compiler_params=pltpu.CompilerParams(vmem_limit_bytes=SIDE_VMEM),
        name="pack",
    )(dest, lens, table, cache, *after)


def relay_body(*refs):
    out_ref, buf, sem_in, sem_out = refs[-4:]
    ins = refs[: out_ref.shape[0]]
    for i, ref in enumerate(ins):
        pltpu.make_async_copy(ref.at[ref.shape[0] - 1], buf.at[i], sem_in.at[i]).start()
    for i, ref in enumerate(ins):
        pltpu.make_async_copy(ref.at[ref.shape[0] - 1], buf.at[i], sem_in.at[i]).wait()
        pltpu.make_async_copy(buf.at[i], out_ref.at[i], sem_out.at[i]).start()
    for i, ref in enumerate(ins):
        pltpu.make_async_copy(buf.at[i], out_ref.at[i], sem_out.at[i]).wait()


def relay(arrays, after):
    shape = (len(arrays),) + arrays[0].shape[1:]
    return pl.pallas_call(
        relay_body,
        out_shape=jax.ShapeDtypeStruct(shape, arrays[0].dtype),
        in_specs=[hbm()] * (len(arrays) + len(after)),
        out_specs=hbm(),
        scratch_shapes=[
            pltpu.VMEM(shape, arrays[0].dtype),
            pltpu.SemaphoreType.DMA((len(arrays),)),
            pltpu.SemaphoreType.DMA((len(arrays),)),
        ],
        compiler_params=pltpu.CompilerParams(vmem_limit_bytes=SIDE_VMEM),
        name="relay",
    )(*arrays, *after)


def place(table, arrays, sources, shape, first, made=(), absolute=False):
    per = table.shape[1]
    tail = arrays[0].shape[2:]
    moves = [(which, e, hop, j) for which, e, hop in sources for j in range(per)]
    count = len(moves)

    def body(table_ref, *refs):
        ins = refs[: len(arrays)]
        out_ref, buf, sem_in, sem_out = refs[-4:]
        me = 0 if absolute else lax.axis_index("seq")

        def fetch(i, which, e, j):
            return pltpu.make_async_copy(ins[which].at[e, j], buf.at[i], sem_in.at[i])

        def ship(i, hop, j):
            row = table_ref[0, j, hop if absolute else jnp.bitwise_xor(me, hop)]
            return pltpu.make_async_copy(
                buf.at[i], out_ref.at[row, pl.ds(first, tail[0])], sem_out.at[i]
            )

        for i, (which, e, hop, j) in enumerate(moves):
            fetch(i, which, e, j).start()
        for i, (which, e, hop, j) in enumerate(moves):
            fetch(i, which, e, j).wait()
            ship(i, hop, j).start()
        for i, (which, e, hop, j) in enumerate(moves):
            ship(i, hop, j).wait()

    return pl.pallas_call(
        body,
        out_shape=jax.ShapeDtypeStruct(shape, arrays[0].dtype),
        in_specs=[smem()] + [hbm()] * (len(arrays) + len(made)),
        out_specs=hbm(),
        scratch_shapes=[
            pltpu.VMEM((count,) + tail, arrays[0].dtype),
            pltpu.SemaphoreType.DMA((count,)),
            pltpu.SemaphoreType.DMA((count,)),
        ],
        input_output_aliases={1 + len(arrays): 0} if made else {},
        compiler_params=pltpu.CompilerParams(vmem_limit_bytes=SIDE_VMEM),
        name="place",
    )(table, *arrays, *made)


def place_last(table, arrays, hops, made):
    per = table.shape[1]
    moves = [(which, hop, j) for which, hop in enumerate(hops) for j in range(per)]

    def body(table_ref, *refs):
        out_ref, sem = refs[-2:]
        me = lax.axis_index("seq")

        def ship(i, which, hop, j):
            row = table_ref[0, j, jnp.bitwise_xor(me, hop)]
            return pltpu.make_async_copy(
                refs[which].at[0, j], out_ref.at[row, pl.ds(0, arrays[0].shape[2])], sem.at[i]
            )

        for i, move in enumerate(moves):
            ship(i, *move).start()
        for i, move in enumerate(moves):
            ship(i, *move).wait()

    return pl.pallas_call(
        body,
        out_shape=jax.ShapeDtypeStruct(made.shape, made.dtype),
        in_specs=[smem()] + [vmem()] * len(arrays) + [hbm()],
        out_specs=hbm(),
        scratch_shapes=[pltpu.SemaphoreType.DMA((len(moves),))],
        input_output_aliases={1 + len(arrays): 0},
        compiler_params=pltpu.CompilerParams(vmem_limit_bytes=4 << 20),
        name="place_last",
    )(table, *arrays, made)


def layer_body(ways, q_heads, kv_heads, *refs):
    (span_ref, lens_ref, table_ref, inv_ref) = refs[:4]
    gains = refs[4 : 4 + ways]
    xs = refs[4 + ways : 4 + 2 * ways]
    wq_ref, wk_ref, wv_ref, wo_ref, cache_ref = refs[4 + 2 * ways : 9 + 2 * ways]
    base_ref = refs[9 + 2 * ways]
    sends = refs[10 + 2 * ways : 9 + 3 * ways]
    (
        x_s, nrm_s, wq_s, wk_s, wv_s, wo_s, kv_s, acc_s, q_s, k_s, v_s, att_s, flat_s,
        cos_s, low_s, high_s, x_sem, w_sem, o_sem, kv_sem,
    ) = refs[9 + 3 * ways :]
    rows, feats = xs[0].shape
    per, reqs = table_ref.shape[1], table_ref.shape[2]
    block_len = cache_ref.shape[-1]
    group = q_heads // kv_heads
    me = lax.axis_index("tp")

    def x_copy(t):
        return pltpu.make_async_copy(xs[t], x_s.at[t], x_sem.at[t])

    w_copies = [
        pltpu.make_async_copy(wq_ref, wq_s, w_sem.at[0]),
        pltpu.make_async_copy(wk_ref, wk_s, w_sem.at[1]),
        pltpu.make_async_copy(wv_ref, wv_s, w_sem.at[2]),
    ]

    def o_copy(t):
        col = pl.multiple_of(lax.rem(me + t, ways) * feats, LANES)
        return pltpu.make_async_copy(wo_ref.at[:, pl.ds(col, feats)], wo_s.at[t], o_sem.at[t])

    def kv_copy(r, j):
        return pltpu.make_async_copy(
            cache_ref.at[table_ref[0, j, r]],
            kv_s.at[r, :, :, pl.ds(0, HEAD_DIM), pl.ds(j * block_len, block_len)],
            kv_sem.at[r * per + j],
        )

    for t in range(ways):
        x_copy(t).start()
    for copy in w_copies:
        copy.start()

    def kv_start(r, carry):
        for j in range(per):
            kv_copy(r, j).start()
        return carry

    lax.fori_loop(0, reqs, kv_start, 0)
    for t in range(ways):
        o_copy(t).start()

    row_id = lax.broadcasted_iota(jnp.int32, (rows, LANES), 0)

    def shift_of(r, carry):
        offset, shift = carry
        shift = jnp.where(row_id >= offset, lens_ref[0, r] - offset, shift)
        return offset + span_ref[0, r], shift

    _, shift = lax.fori_loop(0, reqs, shift_of, (jnp.int32(0), jnp.zeros_like(row_id)))
    angle = (row_id + shift).astype(jnp.float32) * inv_ref[...]
    lane = lax.broadcasted_iota(jnp.int32, (rows, LANES), 1)
    cos_s[...] = jnp.where(lane < HEAD_DIM, jnp.cos(angle), 0.0)
    sine = jnp.sin(angle)
    low_s[...] = jnp.where(lane < HALF, -sine, 0.0)
    high_s[...] = jnp.where((lane >= HALF) & (lane < HEAD_DIM), sine, 0.0)

    pad = kv_s.shape[3] - HEAD_DIM
    zeros_kv = jnp.zeros((2, pad, kv_s.shape[4]), kv_s.dtype)

    def kv_zero(r, carry):
        for g in range(kv_heads):
            kv_s[r, g, :, HEAD_DIM:, :] = zeros_kv
        return carry

    lax.fori_loop(0, reqs, kv_zero, 0)
    acc_s[...] = jnp.zeros(acc_s.shape, acc_s.dtype)

    for t in range(ways):
        x_copy(t).wait()
    step = 64

    def norm_rows(m, carry):
        here = pl.ds(pl.multiple_of(m * step, step), step)
        wide = [x_s[t, here, :].astype(jnp.float32) for t in range(ways)]
        total = sum(jnp.sum(w * w, axis=1, keepdims=True) for w in wide)
        scale = lax.rsqrt(total / (ways * feats) + EPS)
        for t in range(ways):
            nrm_s[lax.rem(me + t, ways), here, :] = (
                wide[t] * scale * gains[t][...].astype(jnp.float32)
            ).astype(jnp.bfloat16)
        return carry

    lax.fori_loop(0, rows // step, norm_rows, 0)

    tall = 256

    def project(w_s, first, width, here):
        total = None
        for c in range(ways):
            deep = slice(c * feats, (c + 1) * feats)
            if first is None:
                part = lax.dot_general(
                    nrm_s[c, here, :], w_s[:, deep], NT, preferred_element_type=jnp.float32
                )
            else:
                part = jnp.dot(
                    nrm_s[c, here, :], w_s[deep, first : first + width],
                    preferred_element_type=jnp.float32,
                )
            total = part if total is None else total + part
        acc_s[:, :width] = total

    def head_of(h):
        base = HEAD_DIM * h // LANES * LANES
        shift = HEAD_DIM * h - base
        wide = acc_s[:, base : base + 2 * LANES]
        if shift:
            wide = pltpu.roll(wide, 2 * LANES - shift, 1)
        return wide[:, :LANES]

    def rotated(h, here):
        value = head_of(h)
        return (
            value * cos_s[here, :]
            + pltpu.roll(value, LANES - HALF, 1) * low_s[here, :]
            + pltpu.roll(value, HALF, 1) * high_s[here, :]
        ).astype(jnp.bfloat16)

    for copy in w_copies:
        copy.wait()
    block_heads = min(8, q_heads)

    def project_rows(m, carry):
        here = pl.ds(pl.multiple_of(m * tall, tall), tall)
        project(wk_s, None, kv_heads * HEAD_DIM, here)
        for g in range(kv_heads):
            k_s[g, here, :] = rotated(g, here)
        project(wv_s, None, kv_heads * HEAD_DIM, here)
        narrow = lax.broadcasted_iota(jnp.int32, (tall, LANES), 1) < HEAD_DIM
        for g in range(kv_heads):
            v_s[g, here, :] = jnp.where(narrow, head_of(g), 0.0).astype(jnp.bfloat16)
        for block in range(q_heads // block_heads):
            project(wq_s, block * block_heads * HEAD_DIM, block_heads * HEAD_DIM, here)
            for h in range(block_heads):
                q_s[block * block_heads + h, here, :] = rotated(h, here)
        return carry

    lax.fori_loop(0, rows // tall, project_rows, 0)

    log_scale = (1.0 / math.sqrt(HEAD_DIM)) * math.log2(math.e)
    keys_old = per * block_len

    def request(r, offset):
        span = span_ref[0, r]
        prior = lens_ref[0, r]
        for j in range(per):
            kv_copy(r, j).wait()
        first = offset // 16 * 16
        key_first = pl.multiple_of(jnp.minimum(first, rows - LANES), 16)
        old_ok = lax.broadcasted_iota(jnp.int32, (1, keys_old), 1) < prior

        def tile(i, carry):
            begin = pl.multiple_of(first + i * ROWS, 16)
            here = pl.ds(begin, ROWS)
            row = begin + lax.broadcasted_iota(jnp.int32, (ROWS, LANES), 0)
            key = key_first + lax.broadcasted_iota(jnp.int32, (ROWS, LANES), 1)
            new_ok = ((key <= row) & (key >= offset))[None]
            keep = ((row >= offset) & (row < offset + span))[None]
            scores = []
            for g in range(kv_heads):
                heads = slice(g * group, (g + 1) * group)
                query = q_s[heads, here, :].reshape(group * ROWS, LANES)
                old = jnp.dot(query, kv_s[r, g, 0], preferred_element_type=jnp.float32)
                new = lax.dot_general(
                    query, k_s[g, pl.ds(key_first, LANES), :], NT,
                    preferred_element_type=jnp.float32,
                )
                scores.append((old, new))
            probs = []
            for old, new in scores:
                old = jnp.where(old_ok, old, MASKED)
                new = jnp.where(new_ok, new.reshape(group, ROWS, LANES), MASKED)
                new = new.reshape(group * ROWS, LANES)
                wide = jnp.maximum(jnp.maximum(old[:, :LANES], old[:, LANES:]), new)
                top = jnp.max(wide, axis=1, keepdims=True)
                old = jnp.exp2((old - top) * log_scale)
                new = jnp.exp2((new - top) * log_scale)
                wide = old[:, :LANES] + old[:, LANES:] + new
                total = jnp.sum(wide, axis=1, keepdims=True)
                probs.append((old.astype(jnp.bfloat16), new.astype(jnp.bfloat16), total))
            for g in range(kv_heads):
                heads = slice(g * group, (g + 1) * group)
                old, new, total = probs[g]
                mixed = lax.dot_general(
                    old, kv_s[r, g, 1], NT, preferred_element_type=jnp.float32,
                ) + jnp.dot(
                    new, v_s[g, pl.ds(key_first, LANES), :],
                    preferred_element_type=jnp.float32,
                )
                mixed = (mixed / total).reshape(group, ROWS, LANES)
                att_s[heads, here, :] = jnp.where(keep, mixed, att_s[heads, here, :])
            return carry

        lax.fori_loop(0, (offset - first + span + ROWS - 1) // ROWS, tile, 0)
        return offset + span

    lax.fori_loop(0, reqs, request, jnp.int32(0))

    for t in range(ways):
        o_copy(t).wait()

    def out_rows(m, carry):
        here = pl.ds(pl.multiple_of(m * tall, tall), tall)
        flat_s[...] = jnp.zeros(flat_s.shape, flat_s.dtype)
        for h in range(q_heads):
            base = HEAD_DIM * h // LANES * LANES
            shift = HEAD_DIM * h - base
            value = att_s[h, here, :]
            wide = jnp.concatenate([value, jnp.zeros_like(value)], axis=1)
            if shift:
                wide = pltpu.roll(wide, shift, 1)
            flat_s[:, base : base + 2 * LANES] += wide
        flat = flat_s[:, : q_heads * HEAD_DIM].astype(jnp.bfloat16)
        for t in range(ways):
            part = jnp.dot(flat, wo_s[t], preferred_element_type=jnp.float32)
            if t == 0:
                base_ref[here, :] = x_s[0, here, :].astype(jnp.float32) + part
            else:
                sends[t - 1][here, :] = part.astype(jnp.bfloat16)
        return carry

    lax.fori_loop(0, rows // tall, out_rows, 0)


def layer(ways, spans, lens, table, gains, xs, w_query, w_key, w_value, w_out, cache):
    rows, feats = xs[0].shape
    q_heads = w_query.shape[1] // HEAD_DIM
    kv_heads = w_key.shape[0] // HEAD_DIM
    per, reqs = table.shape[1], table.shape[2]
    keys = per * cache.shape[-1]
    pairs = np.arange(LANES) % HALF
    inverse = np.where(
        np.arange(LANES) < HEAD_DIM, np.float64(THETA) ** (-2.0 * pairs / HEAD_DIM), 0.0
    ).astype(np.float32)[None]
    bf, f32 = jnp.bfloat16, jnp.float32
    outs = pl.pallas_call(
        functools.partial(layer_body, ways, q_heads, kv_heads),
        out_shape=[jax.ShapeDtypeStruct((rows, feats), f32)]
        + [jax.ShapeDtypeStruct((rows, feats), bf)] * (ways - 1),
        in_specs=[smem(), smem(), smem(), vmem()] + [vmem()] * ways + [hbm()] * (ways + 5),
        out_specs=[vmem()] * ways,
        scratch_shapes=[
            pltpu.VMEM((ways, rows, feats), bf),
            pltpu.VMEM((ways, rows, feats), bf),
            pltpu.VMEM(w_query.shape, bf),
            pltpu.VMEM(w_key.shape, bf),
            pltpu.VMEM(w_value.shape, bf),
            pltpu.VMEM((ways, w_out.shape[0], feats), bf),
            pltpu.VMEM((reqs, kv_heads, 2, LANES, keys), bf),
            pltpu.VMEM((256, min(8, q_heads) * HEAD_DIM + LANES), f32),
            pltpu.VMEM((q_heads, rows + ROWS, LANES), bf),
            pltpu.VMEM((kv_heads, rows, LANES), bf),
            pltpu.VMEM((kv_heads, rows, LANES), bf),
            pltpu.VMEM((q_heads, rows + ROWS, LANES), f32),
            pltpu.VMEM((256, q_heads * HEAD_DIM + LANES), f32),
            pltpu.VMEM((rows, LANES), f32),
            pltpu.VMEM((rows, LANES), f32),
            pltpu.VMEM((rows, LANES), f32),
            pltpu.SemaphoreType.DMA((ways,)),
            pltpu.SemaphoreType.DMA((3,)),
            pltpu.SemaphoreType.DMA((ways,)),
            pltpu.SemaphoreType.DMA((reqs * per,)),
        ],
        compiler_params=pltpu.CompilerParams(vmem_limit_bytes=LAYER_VMEM),
        cost_estimate=pl.CostEstimate(
            flops=100 * 2 * rows * ways * feats * 2 * w_query.shape[1],
            transcendentals=0,
            bytes_accessed=4 * w_query.size,
        ),
        name="layer",
    )(spans, lens, table, jnp.asarray(inverse), *gains, *xs, w_query, w_key, w_value, w_out, cache)
    return outs[0], outs[1:]


def local(
    tokens,
    norm_gain,
    w_query,
    w_key,
    w_value,
    w_out,
    prior_cache,
    prior_lens,
    span_lens,
    prior_table,
    dest_device,
    dest_table,
):
    ways = lax.axis_size("tp")
    w_key, w_value = w_key.T, w_value.T
    prior_table = prior_table.transpose(0, 2, 1)
    dest_table = dest_table.transpose(0, 2, 1)
    def from_peer(value, t):
        return lax.ppermute(value, "tp", [((d + t) % ways, d) for d in range(ways)])

    def to_peer(value, t):
        return lax.ppermute(value, "tp", [(d, (d + t) % ways) for d in range(ways)])

    peers = lax.axis_size("seq")
    pairs = peers // 2

    def to_hop(value, hop):
        return lax.ppermute(value, "seq", [(d, d ^ hop) for d in range(peers)])

    barrier = lax.optimization_barrier
    far = list(range(pairs // 2, pairs))
    near = list(range(1, pairs // 2))
    pair = lambda k: (2 * k, 2 * k + 1)
    begin = far[:2] + near[:1]
    middle = near[1:]
    late = [hop for k in far[2:] for hop in pair(k)]
    args = (dest_device, prior_lens, prior_table, prior_cache)
    heads = prior_cache.shape[1]
    few = max(1, heads * BY_PERMUTE // 4)
    xs = [tokens] + [from_peer(tokens, t) for t in range(1, ways)]
    begin_out = pack([pair(k) for k in begin], *args, [], 0, few)
    (bulk_out,) = pack(
        [tuple(range(peers))], *args, begin_out[-1:], few, heads - few, absolute=True
    )
    hops = [pair(k) for k in middle] + [(hop,) for hop in late] + [(0, 1)]
    rest = pack(hops, *args, [bulk_out], 0, few)
    middle_out, late_out, own = rest[: len(middle)], rest[len(middle) : -1], rest[-1]
    begin_in = [to_hop(value, 2 * k) for k, value in zip(begin, begin_out)]
    bulk_in = lax.all_to_all(bulk_out, "seq", split_axis=0, concat_axis=0, tiled=True)
    gain = barrier((norm_gain, bulk_out))[0][None, :]
    gains = [gain] + [from_peer(gain, t) for t in range(1, ways)]
    xs, begin_in = barrier((xs, begin_in))
    base, sends = layer(
        ways, span_lens, prior_lens, prior_table, gains, xs,
        w_query, w_key, w_value, w_out, prior_cache,
    )
    sends, middle_out, late_out = barrier((sends, middle_out, late_out))
    middle_in = [to_hop(value, 2 * k) for k, value in zip(middle, middle_out)]
    late_in = [to_hop(value, hop) for hop, value in zip(late, late_out)]
    total = base
    for t in range(1, ways):
        total = total + to_peer(sends[t - 1], t).astype(jnp.float32)
    hidden = total.astype(jnp.bfloat16)

    arrived = begin_in + middle_in
    other = to_hop(relay(arrived + [own], [hidden]), 1)
    reach = [2 * k for k in begin + middle] + [0]
    sources = [(i, 0, hop) for i, hop in enumerate(reach)]
    sources += [(len(reach), i, hop + 1) for i, hop in enumerate(reach)]
    shape = prior_cache.shape
    made = place(dest_table, arrived + [own, other], sources, shape, 0)
    bulk = [(0, s, s) for s in range(peers)]
    made = place(dest_table, [bulk_in], bulk, shape, few, [made], absolute=True)
    decode_cache = place_last(dest_table, late_in, late, made)
    return (hidden, decode_cache)


def solution(mesh):
    in_specs = (
        P("seq", "tp"),
        P("tp"),
        P(None, "tp"),
        P(None, "tp"),
        P(None, "tp"),
        P("tp", None),
        P("seq", "tp", None, None, None),
        P("seq", None),
        P("seq", None),
        P("seq", None, None),
        P("seq", None),
        P("seq", None, None),
    )
    out_specs = (P("seq", "tp"), P("seq", "tp", None, None, None))
    return jax.shard_map(local, mesh=mesh, in_specs=in_specs, out_specs=out_specs, check_vma=False)
```

```python
import functools
import math

import jax
import jax.numpy as jnp
import numpy as np
from jax import lax
from jax.experimental import pallas as pl
from jax.experimental.pallas import tpu as pltpu
from jax.sharding import PartitionSpec as P

HEAD_DIM = 80
HALF = HEAD_DIM // 2
LANES = 128
WINDOW = 64
EPS = 1e-05
THETA = 1000000.0
MASKED = -1e30
ROWS = 64
BY_PERMUTE = 1
SIDE_VMEM = 62 << 20
LAYER_VMEM = 62 << 20
NT = (((1,), (1,)), ((), ()))


def smem():
    return pl.BlockSpec(memory_space=pltpu.SMEM)


def vmem():
    return pl.BlockSpec(memory_space=pltpu.VMEM)


def hbm():
    return pl.BlockSpec(memory_space=pl.ANY)


def pack_body(hops, first, absolute, dest_ref, lens_ref, table_ref, cache_ref, *refs):
    outs = refs[: len(hops)]
    inverse, buf, sem_in, sem_out = refs[-4:]
    reqs = dest_ref.shape[1]
    per = table_ref.shape[1]
    block_len = cache_ref.shape[-1]
    me = 0 if absolute else lax.axis_index("seq")
    heads = outs[0].shape[2]

    def invert(r, carry):
        inverse[dest_ref[0, r]] = r
        return carry

    lax.fori_loop(0, reqs, invert, 0)
    steps = []
    for ref, group in zip(outs, hops):
        for e, hop in enumerate(group):
            for j in range(per):
                steps.append((len(steps), ref, e, hop, j))

    def toward(hop):
        return hop if absolute else jnp.bitwise_xor(me, hop)

    def count_of(hop, j):
        return lens_ref[0, inverse[toward(hop)]] - j * block_len

    def fetch(i, hop, j):
        row = table_ref[0, j, inverse[toward(hop)]]
        return pltpu.make_async_copy(
            cache_ref.at[row, pl.ds(first, heads)], buf.at[i], sem_in.at[i]
        )

    def ship(i, ref, e, j):
        return pltpu.make_async_copy(buf.at[i], ref.at[e, j], sem_out.at[i])

    for i, ref, e, hop, j in steps:
        @pl.when(count_of(hop, j) > 0)
        def _():
            fetch(i, hop, j).start()

    for i, ref, e, hop, j in steps:
        count = count_of(hop, j)

        @pl.when(count > 0)
        def _():
            fetch(i, hop, j).wait()

        @pl.when(count < block_len)
        def _():
            block = buf[i]
            lane = lax.broadcasted_iota(jnp.int32, block.shape, block.ndim - 1)
            buf[i] = jnp.where(lane < count, block.astype(jnp.float32), 0.0).astype(jnp.bfloat16)

        ship(i, ref, e, j).start()

    for i, ref, e, hop, j in steps:
        ship(i, ref, e, j).wait()


def pack(hops, dest, lens, table, cache, after, first, heads, absolute=False):
    per, reqs = table.shape[1], table.shape[2]
    count = sum(len(group) for group in hops) * per
    tail = (heads,) + cache.shape[2:]

    def body(*refs):
        pack_body(hops, first, absolute, *refs[:4], *refs[4 + len(after) :])

    return pl.pallas_call(
        body,
        out_shape=[jax.ShapeDtypeStruct((len(group), per) + tail, cache.dtype) for group in hops],
        in_specs=[smem(), smem(), smem(), hbm()] + [hbm()] * len(after),
        out_specs=[hbm()] * len(hops),
        scratch_shapes=[
            pltpu.SMEM((reqs,), jnp.int32),
            pltpu.VMEM((count,) + tail, cache.dtype),
            pltpu.SemaphoreType.DMA((count,)),
            pltpu.SemaphoreType.DMA((count,)),
        ],
        compiler_params=pltpu.CompilerParams(vmem_limit_bytes=SIDE_VMEM),
        name="pack",
    )(dest, lens, table, cache, *after)


def relay_body(*refs):
    out_ref, buf, sem_in, sem_out = refs[-4:]
    ins = refs[: out_ref.shape[0]]
    for i, ref in enumerate(ins):
        pltpu.make_async_copy(ref.at[ref.shape[0] - 1], buf.at[i], sem_in.at[i]).start()
    for i, ref in enumerate(ins):
        pltpu.make_async_copy(ref.at[ref.shape[0] - 1], buf.at[i], sem_in.at[i]).wait()
        pltpu.make_async_copy(buf.at[i], out_ref.at[i], sem_out.at[i]).start()
    for i, ref in enumerate(ins):
        pltpu.make_async_copy(buf.at[i], out_ref.at[i], sem_out.at[i]).wait()


def relay(arrays, after):
    shape = (len(arrays),) + arrays[0].shape[1:]
    return pl.pallas_call(
        relay_body,
        out_shape=jax.ShapeDtypeStruct(shape, arrays[0].dtype),
        in_specs=[hbm()] * (len(arrays) + len(after)),
        out_specs=hbm(),
        scratch_shapes=[
            pltpu.VMEM(shape, arrays[0].dtype),
            pltpu.SemaphoreType.DMA((len(arrays),)),
            pltpu.SemaphoreType.DMA((len(arrays),)),
        ],
        compiler_params=pltpu.CompilerParams(vmem_limit_bytes=SIDE_VMEM),
        name="relay",
    )(*arrays, *after)


def place(table, arrays, sources, bulk, shape):
    per = table.shape[1]
    tail, bulk_tail = arrays[0].shape[2:], bulk.shape[2:]
    moves = [(which, e, hop, j) for which, e, hop in sources for j in range(per)]
    bulk_moves = [(s, j) for s in range(bulk.shape[0]) for j in range(per)]
    count, bulk_count = len(moves), len(bulk_moves)

    def body(table_ref, *refs):
        bulk_ref = refs[len(arrays)]
        out_ref, buf, bulk_buf, sem_in, sem_out, bulk_sem_in, bulk_sem_out = refs[-7:]
        me = lax.axis_index("seq")

        def fetch(i, which, e, j):
            return pltpu.make_async_copy(refs[which].at[e, j], buf.at[i], sem_in.at[i])

        def ship(i, hop, j):
            row = table_ref[0, j, jnp.bitwise_xor(me, hop)]
            return pltpu.make_async_copy(
                buf.at[i], out_ref.at[row, pl.ds(0, tail[0])], sem_out.at[i]
            )

        def bulk_fetch(i, s, j):
            return pltpu.make_async_copy(bulk_ref.at[s, j], bulk_buf.at[i], bulk_sem_in.at[i])

        def bulk_ship(i, s, j):
            return pltpu.make_async_copy(
                bulk_buf.at[i],
                out_ref.at[table_ref[0, j, s], pl.ds(tail[0], bulk_tail[0])],
                bulk_sem_out.at[i],
            )

        for i, move in enumerate(bulk_moves):
            bulk_fetch(i, *move).start()
        for i, (which, e, hop, j) in enumerate(moves):
            fetch(i, which, e, j).start()
        for i, move in enumerate(bulk_moves):
            bulk_fetch(i, *move).wait()
            bulk_ship(i, *move).start()
        for i, (which, e, hop, j) in enumerate(moves):
            fetch(i, which, e, j).wait()
            ship(i, hop, j).start()
        for i, move in enumerate(bulk_moves):
            bulk_ship(i, *move).wait()
        for i, (which, e, hop, j) in enumerate(moves):
            ship(i, hop, j).wait()

    return pl.pallas_call(
        body,
        out_shape=jax.ShapeDtypeStruct(shape, bulk.dtype),
        in_specs=[smem()] + [hbm()] * (len(arrays) + 1),
        out_specs=hbm(),
        scratch_shapes=[
            pltpu.VMEM((count,) + tail, bulk.dtype),
            pltpu.VMEM((bulk_count,) + bulk_tail, bulk.dtype),
            pltpu.SemaphoreType.DMA((count,)),
            pltpu.SemaphoreType.DMA((count,)),
            pltpu.SemaphoreType.DMA((bulk_count,)),
            pltpu.SemaphoreType.DMA((bulk_count,)),
        ],
        compiler_params=pltpu.CompilerParams(vmem_limit_bytes=SIDE_VMEM),
        name="place",
    )(table, *arrays, bulk)


def place_last(table, arrays, hops, made):
    per = table.shape[1]
    moves = [(which, hop, j) for which, hop in enumerate(hops) for j in range(per)]

    def body(table_ref, *refs):
        out_ref, sem = refs[-2:]
        me = lax.axis_index("seq")

        def ship(i, which, hop, j):
            row = table_ref[0, j, jnp.bitwise_xor(me, hop)]
            return pltpu.make_async_copy(
                refs[which].at[0, j], out_ref.at[row, pl.ds(0, arrays[0].shape[2])], sem.at[i]
            )

        for i, move in enumerate(moves):
            ship(i, *move).start()
        for i, move in enumerate(moves):
            ship(i, *move).wait()

    return pl.pallas_call(
        body,
        out_shape=jax.ShapeDtypeStruct(made.shape, made.dtype),
        in_specs=[smem()] + [vmem()] * len(arrays) + [hbm()],
        out_specs=hbm(),
        scratch_shapes=[pltpu.SemaphoreType.DMA((len(moves),))],
        input_output_aliases={1 + len(arrays): 0},
        compiler_params=pltpu.CompilerParams(vmem_limit_bytes=4 << 20),
        name="place_last",
    )(table, *arrays, made)


def layer_body(ways, q_heads, kv_heads, *refs):
    (span_ref, lens_ref, table_ref, inv_ref) = refs[:4]
    gains = refs[4 : 4 + ways]
    xs = refs[4 + ways : 4 + 2 * ways]
    wq_ref, wk_ref, wv_ref, wo_ref, cache_ref = refs[4 + 2 * ways : 9 + 2 * ways]
    base_ref = refs[9 + 2 * ways]
    sends = refs[10 + 2 * ways : 9 + 3 * ways]
    (
        x_s, nrm_s, wq_s, wk_s, wv_s, wo_s, kv_s, acc_s, q_s, k_s, v_s, att_s, flat_s,
        cos_s, low_s, high_s, x_sem, w_sem, o_sem, kv_sem,
    ) = refs[9 + 3 * ways :]
    rows, feats = xs[0].shape
    per, reqs = table_ref.shape[1], table_ref.shape[2]
    block_len = cache_ref.shape[-1]
    group = q_heads // kv_heads
    me = lax.axis_index("tp")

    def x_copy(t):
        return pltpu.make_async_copy(xs[t], x_s.at[t], x_sem.at[t])

    w_copies = [
        pltpu.make_async_copy(wq_ref, wq_s, w_sem.at[0]),
        pltpu.make_async_copy(wk_ref, wk_s, w_sem.at[1]),
        pltpu.make_async_copy(wv_ref, wv_s, w_sem.at[2]),
    ]

    def o_copy(t):
        col = pl.multiple_of(lax.rem(me + t, ways) * feats, LANES)
        return pltpu.make_async_copy(wo_ref.at[:, pl.ds(col, feats)], wo_s.at[t], o_sem.at[t])

    def kv_copy(r, j):
        return pltpu.make_async_copy(
            cache_ref.at[table_ref[0, j, r]],
            kv_s.at[r, :, :, pl.ds(0, HEAD_DIM), pl.ds(j * block_len, block_len)],
            kv_sem.at[r * per + j],
        )

    for t in range(ways):
        x_copy(t).start()
    for copy in w_copies:
        copy.start()

    def kv_start(r, carry):
        for j in range(per):
            kv_copy(r, j).start()
        return carry

    lax.fori_loop(0, reqs, kv_start, 0)
    for t in range(ways):
        o_copy(t).start()

    row_id = lax.broadcasted_iota(jnp.int32, (rows, LANES), 0)

    def shift_of(r, carry):
        offset, shift = carry
        shift = jnp.where(row_id >= offset, lens_ref[0, r] - offset, shift)
        return offset + span_ref[0, r], shift

    _, shift = lax.fori_loop(0, reqs, shift_of, (jnp.int32(0), jnp.zeros_like(row_id)))
    angle = (row_id + shift).astype(jnp.float32) * inv_ref[...]
    lane = lax.broadcasted_iota(jnp.int32, (rows, LANES), 1)
    cos_s[...] = jnp.where(lane < HEAD_DIM, jnp.cos(angle), 0.0)
    sine = jnp.sin(angle)
    low_s[...] = jnp.where(lane < HALF, -sine, 0.0)
    high_s[...] = jnp.where((lane >= HALF) & (lane < HEAD_DIM), sine, 0.0)

    pad = kv_s.shape[3] - HEAD_DIM
    zeros_kv = jnp.zeros((2, pad, kv_s.shape[4]), kv_s.dtype)

    def kv_zero(r, carry):
        for g in range(kv_heads):
            kv_s[r, g, :, HEAD_DIM:, :] = zeros_kv
        return carry

    lax.fori_loop(0, reqs, kv_zero, 0)
    acc_s[...] = jnp.zeros(acc_s.shape, acc_s.dtype)

    for t in range(ways):
        x_copy(t).wait()
    step = 64

    def norm_rows(m, carry):
        here = pl.ds(pl.multiple_of(m * step, step), step)
        wide = [x_s[t, here, :].astype(jnp.float32) for t in range(ways)]
        total = sum(jnp.sum(w * w, axis=1, keepdims=True) for w in wide)
        scale = lax.rsqrt(total / (ways * feats) + EPS)
        for t in range(ways):
            nrm_s[lax.rem(me + t, ways), here, :] = (
                wide[t] * scale * gains[t][...].astype(jnp.float32)
            ).astype(jnp.bfloat16)
        return carry

    lax.fori_loop(0, rows // step, norm_rows, 0)

    tall = 256

    def project(w_s, first, width, here):
        total = None
        for c in range(ways):
            deep = slice(c * feats, (c + 1) * feats)
            if first is None:
                part = lax.dot_general(
                    nrm_s[c, here, :], w_s[:, deep], NT, preferred_element_type=jnp.float32
                )
            else:
                part = jnp.dot(
                    nrm_s[c, here, :], w_s[deep, first : first + width],
                    preferred_element_type=jnp.float32,
                )
            total = part if total is None else total + part
        acc_s[:, :width] = total

    def head_of(h):
        base = HEAD_DIM * h // LANES * LANES
        shift = HEAD_DIM * h - base
        wide = acc_s[:, base : base + 2 * LANES]
        if shift:
            wide = pltpu.roll(wide, 2 * LANES - shift, 1)
        return wide[:, :LANES]

    def rotated(h, here):
        value = head_of(h)
        return (
            value * cos_s[here, :]
            + pltpu.roll(value, LANES - HALF, 1) * low_s[here, :]
            + pltpu.roll(value, HALF, 1) * high_s[here, :]
        ).astype(jnp.bfloat16)

    for copy in w_copies:
        copy.wait()
    block_heads = min(8, q_heads)

    def project_rows(m, carry):
        here = pl.ds(pl.multiple_of(m * tall, tall), tall)
        project(wk_s, None, kv_heads * HEAD_DIM, here)
        for g in range(kv_heads):
            k_s[g, here, :] = rotated(g, here)
        project(wv_s, None, kv_heads * HEAD_DIM, here)
        narrow = lax.broadcasted_iota(jnp.int32, (tall, LANES), 1) < HEAD_DIM
        for g in range(kv_heads):
            v_s[g, here, :] = jnp.where(narrow, head_of(g), 0.0).astype(jnp.bfloat16)
        for block in range(q_heads // block_heads):
            project(wq_s, block * block_heads * HEAD_DIM, block_heads * HEAD_DIM, here)
            for h in range(block_heads):
                q_s[block * block_heads + h, here, :] = rotated(h, here)
        return carry

    lax.fori_loop(0, rows // tall, project_rows, 0)

    log_scale = (1.0 / math.sqrt(HEAD_DIM)) * math.log2(math.e)
    keys_old = per * block_len

    def request(r, offset):
        span = span_ref[0, r]
        prior = lens_ref[0, r]
        for j in range(per):
            kv_copy(r, j).wait()
        first = offset // 16 * 16
        key_first = pl.multiple_of(jnp.minimum(first, rows - LANES), 16)
        old_ok = lax.broadcasted_iota(jnp.int32, (1, keys_old), 1) < prior

        def tile(i, carry):
            begin = pl.multiple_of(first + i * ROWS, 16)
            here = pl.ds(begin, ROWS)
            row = begin + lax.broadcasted_iota(jnp.int32, (ROWS, LANES), 0)
            key = key_first + lax.broadcasted_iota(jnp.int32, (ROWS, LANES), 1)
            new_ok = ((key <= row) & (key >= offset))[None]
            keep = ((row >= offset) & (row < offset + span))[None]
            scores = []
            for g in range(kv_heads):
                heads = slice(g * group, (g + 1) * group)
                query = q_s[heads, here, :].reshape(group * ROWS, LANES)
                old = jnp.dot(query, kv_s[r, g, 0], preferred_element_type=jnp.float32)
                new = lax.dot_general(
                    query, k_s[g, pl.ds(key_first, LANES), :], NT,
                    preferred_element_type=jnp.float32,
                )
                scores.append((old, new))
            probs = []
            for old, new in scores:
                old = jnp.where(old_ok, old, MASKED)
                new = jnp.where(new_ok, new.reshape(group, ROWS, LANES), MASKED)
                new = new.reshape(group * ROWS, LANES)
                wide = jnp.maximum(jnp.maximum(old[:, :LANES], old[:, LANES:]), new)
                top = jnp.max(wide, axis=1, keepdims=True)
                old = jnp.exp2((old - top) * log_scale)
                new = jnp.exp2((new - top) * log_scale)
                wide = old[:, :LANES] + old[:, LANES:] + new
                total = jnp.sum(wide, axis=1, keepdims=True)
                probs.append((old.astype(jnp.bfloat16), new.astype(jnp.bfloat16), total))
            for g in range(kv_heads):
                heads = slice(g * group, (g + 1) * group)
                old, new, total = probs[g]
                mixed = lax.dot_general(
                    old, kv_s[r, g, 1], NT, preferred_element_type=jnp.float32,
                ) + jnp.dot(
                    new, v_s[g, pl.ds(key_first, LANES), :],
                    preferred_element_type=jnp.float32,
                )
                mixed = (mixed / total).reshape(group, ROWS, LANES)
                att_s[heads, here, :] = jnp.where(keep, mixed, att_s[heads, here, :])
            return carry

        lax.fori_loop(0, (offset - first + span + ROWS - 1) // ROWS, tile, 0)
        return offset + span

    lax.fori_loop(0, reqs, request, jnp.int32(0))

    for t in range(ways):
        o_copy(t).wait()

    def out_rows(m, carry):
        here = pl.ds(pl.multiple_of(m * tall, tall), tall)
        flat_s[...] = jnp.zeros(flat_s.shape, flat_s.dtype)
        for h in range(q_heads):
            base = HEAD_DIM * h // LANES * LANES
            shift = HEAD_DIM * h - base
            value = att_s[h, here, :]
            wide = jnp.concatenate([value, jnp.zeros_like(value)], axis=1)
            if shift:
                wide = pltpu.roll(wide, shift, 1)
            flat_s[:, base : base + 2 * LANES] += wide
        flat = flat_s[:, : q_heads * HEAD_DIM].astype(jnp.bfloat16)
        for t in range(ways):
            part = jnp.dot(flat, wo_s[t], preferred_element_type=jnp.float32)
            if t == 0:
                base_ref[here, :] = x_s[0, here, :].astype(jnp.float32) + part
            else:
                sends[t - 1][here, :] = part.astype(jnp.bfloat16)
        return carry

    lax.fori_loop(0, rows // tall, out_rows, 0)


def layer(ways, spans, lens, table, gains, xs, w_query, w_key, w_value, w_out, cache):
    rows, feats = xs[0].shape
    q_heads = w_query.shape[1] // HEAD_DIM
    kv_heads = w_key.shape[0] // HEAD_DIM
    per, reqs = table.shape[1], table.shape[2]
    keys = per * cache.shape[-1]
    pairs = np.arange(LANES) % HALF
    inverse = np.where(
        np.arange(LANES) < HEAD_DIM, np.float64(THETA) ** (-2.0 * pairs / HEAD_DIM), 0.0
    ).astype(np.float32)[None]
    bf, f32 = jnp.bfloat16, jnp.float32
    outs = pl.pallas_call(
        functools.partial(layer_body, ways, q_heads, kv_heads),
        out_shape=[jax.ShapeDtypeStruct((rows, feats), f32)]
        + [jax.ShapeDtypeStruct((rows, feats), bf)] * (ways - 1),
        in_specs=[smem(), smem(), smem(), vmem()] + [vmem()] * ways + [hbm()] * (ways + 5),
        out_specs=[vmem()] * ways,
        scratch_shapes=[
            pltpu.VMEM((ways, rows, feats), bf),
            pltpu.VMEM((ways, rows, feats), bf),
            pltpu.VMEM(w_query.shape, bf),
            pltpu.VMEM(w_key.shape, bf),
            pltpu.VMEM(w_value.shape, bf),
            pltpu.VMEM((ways, w_out.shape[0], feats), bf),
            pltpu.VMEM((reqs, kv_heads, 2, LANES, keys), bf),
            pltpu.VMEM((256, min(8, q_heads) * HEAD_DIM + LANES), f32),
            pltpu.VMEM((q_heads, rows + ROWS, LANES), bf),
            pltpu.VMEM((kv_heads, rows, LANES), bf),
            pltpu.VMEM((kv_heads, rows, LANES), bf),
            pltpu.VMEM((q_heads, rows + ROWS, LANES), f32),
            pltpu.VMEM((256, q_heads * HEAD_DIM + LANES), f32),
            pltpu.VMEM((rows, LANES), f32),
            pltpu.VMEM((rows, LANES), f32),
            pltpu.VMEM((rows, LANES), f32),
            pltpu.SemaphoreType.DMA((ways,)),
            pltpu.SemaphoreType.DMA((3,)),
            pltpu.SemaphoreType.DMA((ways,)),
            pltpu.SemaphoreType.DMA((reqs * per,)),
        ],
        compiler_params=pltpu.CompilerParams(vmem_limit_bytes=LAYER_VMEM),
        cost_estimate=pl.CostEstimate(
            flops=100 * 2 * rows * ways * feats * 2 * w_query.shape[1],
            transcendentals=0,
            bytes_accessed=4 * w_query.size,
        ),
        name="layer",
    )(spans, lens, table, jnp.asarray(inverse), *gains, *xs, w_query, w_key, w_value, w_out, cache)
    return outs[0], outs[1:]


def local(
    tokens,
    norm_gain,
    w_query,
    w_key,
    w_value,
    w_out,
    prior_cache,
    prior_lens,
    span_lens,
    prior_table,
    dest_device,
    dest_table,
):
    ways = lax.axis_size("tp")
    w_key, w_value = w_key.T, w_value.T
    prior_table = prior_table.transpose(0, 2, 1)
    dest_table = dest_table.transpose(0, 2, 1)
    def from_peer(value, t):
        return lax.ppermute(value, "tp", [((d + t) % ways, d) for d in range(ways)])

    def to_peer(value, t):
        return lax.ppermute(value, "tp", [(d, (d + t) % ways) for d in range(ways)])

    peers = lax.axis_size("seq")
    pairs = peers // 2

    def to_hop(value, hop):
        return lax.ppermute(value, "seq", [(d, d ^ hop) for d in range(peers)])

    barrier = lax.optimization_barrier
    far = list(range(pairs // 2, pairs))
    near = list(range(1, pairs // 2))
    pair = lambda k: (2 * k, 2 * k + 1)
    begin = far[:2] + near[:1]
    middle = near[1:]
    late = [hop for k in far[2:] for hop in pair(k)]
    args = (dest_device, prior_lens, prior_table, prior_cache)
    heads = prior_cache.shape[1]
    few = max(1, heads * BY_PERMUTE // 4)
    xs = [tokens] + [from_peer(tokens, t) for t in range(1, ways)]
    begin_out = pack([pair(k) for k in begin], *args, [], 0, few)
    (bulk_out,) = pack(
        [tuple(range(peers))], *args, begin_out[-1:], few, heads - few, absolute=True
    )
    hops = [pair(k) for k in middle] + [(hop,) for hop in late] + [(0, 1)]
    rest = pack(hops, *args, [bulk_out], 0, few)
    middle_out, late_out, own = rest[: len(middle)], rest[len(middle) : -1], rest[-1]
    begin_in = [to_hop(value, 2 * k) for k, value in zip(begin, begin_out)]
    bulk_in = lax.all_to_all(bulk_out, "seq", split_axis=0, concat_axis=0, tiled=True)
    gain = barrier((norm_gain, bulk_out))[0][None, :]
    gains = [gain] + [from_peer(gain, t) for t in range(1, ways)]
    xs, begin_in = barrier((xs, begin_in))
    base, sends = layer(
        ways, span_lens, prior_lens, prior_table, gains, xs,
        w_query, w_key, w_value, w_out, prior_cache,
    )
    sends, middle_out, late_out = barrier((sends, middle_out, late_out))
    middle_in = [to_hop(value, 2 * k) for k, value in zip(middle, middle_out)]
    late_in = [to_hop(value, hop) for hop, value in zip(late, late_out)]
    got = [to_peer(sends[t - 1], t) for t in range(1, ways)]
    total = base
    for value in got:
        total = total + value.astype(jnp.float32)
    hidden = total.astype(jnp.bfloat16)
    arrived = begin_in + middle_in
    other = to_hop(relay(arrived + [own], [hidden]), 1)
    reach = [2 * k for k in begin + middle] + [0]
    sources = [(i, 0, hop) for i, hop in enumerate(reach)]
    sources += [(len(reach), i, hop + 1) for i, hop in enumerate(reach)]
    shape = prior_cache.shape
    made = place(dest_table, arrived + [own, other], sources, bulk_in, shape)
    decode_cache = place_last(dest_table, late_in, late, made)
    return (hidden, decode_cache)


def solution(mesh):
    in_specs = (
        P("seq", "tp"),
        P("tp"),
        P(None, "tp"),
        P(None, "tp"),
        P(None, "tp"),
        P("tp", None),
        P("seq", "tp", None, None, None),
        P("seq", None),
        P("seq", None),
        P("seq", None, None),
        P("seq", None),
        P("seq", None, None),
    )
    out_specs = (P("seq", "tp"), P("seq", "tp", None, None, None))
    return jax.shard_map(local, mesh=mesh, in_specs=in_specs, out_specs=out_specs, check_vma=False)
```

```python
import functools
import math

import jax
import jax.numpy as jnp
import numpy as np
from jax import lax
from jax.experimental import pallas as pl
from jax.experimental.pallas import tpu as pltpu
from jax.sharding import PartitionSpec as P

HEAD_DIM = 80
HALF = HEAD_DIM // 2
LANES = 128
WINDOW = 64
EPS = 1e-05
THETA = 1000000.0
MASKED = -1e30
ROWS = 64
BY_PERMUTE = 1
SIDE_VMEM = 62 << 20
LAYER_VMEM = 62 << 20
NT = (((1,), (1,)), ((), ()))


def smem():
    return pl.BlockSpec(memory_space=pltpu.SMEM)


def vmem():
    return pl.BlockSpec(memory_space=pltpu.VMEM)


def hbm():
    return pl.BlockSpec(memory_space=pl.ANY)


def pack_body(hops, first, absolute, dest_ref, lens_ref, table_ref, cache_ref, *refs):
    outs = refs[: len(hops)]
    inverse, buf, sem_in, sem_out = refs[-4:]
    reqs = dest_ref.shape[1]
    per = table_ref.shape[1]
    block_len = cache_ref.shape[-1]
    me = 0 if absolute else lax.axis_index("seq")
    heads = outs[0].shape[2]

    def invert(r, carry):
        inverse[dest_ref[0, r]] = r
        return carry

    lax.fori_loop(0, reqs, invert, 0)
    steps = []
    for ref, group in zip(outs, hops):
        for e, hop in enumerate(group):
            for j in range(per):
                steps.append((len(steps), ref, e, hop, j))

    def toward(hop):
        return hop if absolute else jnp.bitwise_xor(me, hop)

    def count_of(hop, j):
        return lens_ref[0, inverse[toward(hop)]] - j * block_len

    def fetch(i, hop, j):
        row = table_ref[0, j, inverse[toward(hop)]]
        return pltpu.make_async_copy(
            cache_ref.at[row, pl.ds(first, heads)], buf.at[i], sem_in.at[i]
        )

    def ship(i, ref, e, j):
        return pltpu.make_async_copy(buf.at[i], ref.at[e, j], sem_out.at[i])

    for i, ref, e, hop, j in steps:
        @pl.when(count_of(hop, j) > 0)
        def _():
            fetch(i, hop, j).start()

    for i, ref, e, hop, j in steps:
        count = count_of(hop, j)

        @pl.when(count > 0)
        def _():
            fetch(i, hop, j).wait()

        @pl.when(count < block_len)
        def _():
            block = buf[i]
            lane = lax.broadcasted_iota(jnp.int32, block.shape, block.ndim - 1)
            buf[i] = jnp.where(lane < count, block.astype(jnp.float32), 0.0).astype(jnp.bfloat16)

        ship(i, ref, e, j).start()

    for i, ref, e, hop, j in steps:
        ship(i, ref, e, j).wait()


def pack(hops, dest, lens, table, cache, after, first, heads, absolute=False):
    per, reqs = table.shape[1], table.shape[2]
    count = sum(len(group) for group in hops) * per
    tail = (heads,) + cache.shape[2:]

    def body(*refs):
        pack_body(hops, first, absolute, *refs[:4], *refs[4 + len(after) :])

    return pl.pallas_call(
        body,
        out_shape=[jax.ShapeDtypeStruct((len(group), per) + tail, cache.dtype) for group in hops],
        in_specs=[smem(), smem(), smem(), hbm()] + [hbm()] * len(after),
        out_specs=[hbm()] * len(hops),
        scratch_shapes=[
            pltpu.SMEM((reqs,), jnp.int32),
            pltpu.VMEM((count,) + tail, cache.dtype),
            pltpu.SemaphoreType.DMA((count,)),
            pltpu.SemaphoreType.DMA((count,)),
        ],
        compiler_params=pltpu.CompilerParams(vmem_limit_bytes=SIDE_VMEM),
        name="pack",
    )(dest, lens, table, cache, *after)


def relay_body(*refs):
    out_ref, buf, sem_in, sem_out = refs[-4:]
    ins = refs[: out_ref.shape[0]]
    for i, ref in enumerate(ins):
        pltpu.make_async_copy(ref.at[ref.shape[0] - 1], buf.at[i], sem_in.at[i]).start()
    for i, ref in enumerate(ins):
        pltpu.make_async_copy(ref.at[ref.shape[0] - 1], buf.at[i], sem_in.at[i]).wait()
        pltpu.make_async_copy(buf.at[i], out_ref.at[i], sem_out.at[i]).start()
    for i, ref in enumerate(ins):
        pltpu.make_async_copy(buf.at[i], out_ref.at[i], sem_out.at[i]).wait()


def relay(arrays, after):
    shape = (len(arrays),) + arrays[0].shape[1:]
    return pl.pallas_call(
        relay_body,
        out_shape=jax.ShapeDtypeStruct(shape, arrays[0].dtype),
        in_specs=[hbm()] * (len(arrays) + len(after)),
        out_specs=hbm(),
        scratch_shapes=[
            pltpu.VMEM(shape, arrays[0].dtype),
            pltpu.SemaphoreType.DMA((len(arrays),)),
            pltpu.SemaphoreType.DMA((len(arrays),)),
        ],
        compiler_params=pltpu.CompilerParams(vmem_limit_bytes=SIDE_VMEM),
        name="relay",
    )(*arrays, *after)


def place(table, arrays, sources, shape, first, made=(), absolute=False):
    per = table.shape[1]
    tail = arrays[0].shape[2:]
    moves = [(which, e, hop, j) for which, e, hop in sources for j in range(per)]
    count = len(moves)

    def body(table_ref, *refs):
        ins = refs[: len(arrays)]
        out_ref, buf, sem_in, sem_out = refs[-4:]
        me = 0 if absolute else lax.axis_index("seq")

        def fetch(i, which, e, j):
            return pltpu.make_async_copy(ins[which].at[e, j], buf.at[i], sem_in.at[i])

        def ship(i, hop, j):
            row = table_ref[0, j, hop if absolute else jnp.bitwise_xor(me, hop)]
            return pltpu.make_async_copy(
                buf.at[i], out_ref.at[row, pl.ds(first, tail[0])], sem_out.at[i]
            )

        for i, (which, e, hop, j) in enumerate(moves):
            fetch(i, which, e, j).start()
        for i, (which, e, hop, j) in enumerate(moves):
            fetch(i, which, e, j).wait()
            ship(i, hop, j).start()
        for i, (which, e, hop, j) in enumerate(moves):
            ship(i, hop, j).wait()

    return pl.pallas_call(
        body,
        out_shape=jax.ShapeDtypeStruct(shape, arrays[0].dtype),
        in_specs=[smem()] + [hbm()] * (len(arrays) + len(made)),
        out_specs=hbm(),
        scratch_shapes=[
            pltpu.VMEM((count,) + tail, arrays[0].dtype),
            pltpu.SemaphoreType.DMA((count,)),
            pltpu.SemaphoreType.DMA((count,)),
        ],
        input_output_aliases={1 + len(arrays): 0} if made else {},
        compiler_params=pltpu.CompilerParams(vmem_limit_bytes=SIDE_VMEM),
        name="place",
    )(table, *arrays, *made)


def place_last(table, arrays, hops, made):
    per = table.shape[1]
    moves = [(which, hop, j) for which, hop in enumerate(hops) for j in range(per)]

    def body(table_ref, *refs):
        out_ref, sem = refs[-2:]
        me = lax.axis_index("seq")

        def ship(i, which, hop, j):
            row = table_ref[0, j, jnp.bitwise_xor(me, hop)]
            return pltpu.make_async_copy(
                refs[which].at[0, j], out_ref.at[row, pl.ds(0, arrays[0].shape[2])], sem.at[i]
            )

        for i, move in enumerate(moves):
            ship(i, *move).start()
        for i, move in enumerate(moves):
            ship(i, *move).wait()

    return pl.pallas_call(
        body,
        out_shape=jax.ShapeDtypeStruct(made.shape, made.dtype),
        in_specs=[smem()] + [vmem()] * len(arrays) + [hbm()],
        out_specs=hbm(),
        scratch_shapes=[pltpu.SemaphoreType.DMA((len(moves),))],
        input_output_aliases={1 + len(arrays): 0},
        compiler_params=pltpu.CompilerParams(vmem_limit_bytes=4 << 20),
        name="place_last",
    )(table, *arrays, made)


def layer_body(ways, q_heads, kv_heads, *refs):
    (span_ref, lens_ref, table_ref, inv_ref) = refs[:4]
    gains = refs[4 : 4 + ways]
    xs = refs[4 + ways : 4 + 2 * ways]
    wq_ref, wk_ref, wv_ref, wo_ref, cache_ref = refs[4 + 2 * ways : 9 + 2 * ways]
    base_ref = refs[9 + 2 * ways]
    sends = refs[10 + 2 * ways : 9 + 3 * ways]
    (
        x_s, nrm_s, wq_s, wk_s, wv_s, wo_s, kv_s, acc_s, q_s, k_s, v_s, att_s, flat_s,
        cos_s, low_s, high_s, x_sem, w_sem, o_sem, kv_sem,
    ) = refs[9 + 3 * ways :]
    rows, feats = xs[0].shape
    per, reqs = table_ref.shape[1], table_ref.shape[2]
    block_len = cache_ref.shape[-1]
    group = q_heads // kv_heads
    me = lax.axis_index("tp")

    def x_copy(t):
        return pltpu.make_async_copy(xs[t], x_s.at[t], x_sem.at[t])

    w_copies = [
        pltpu.make_async_copy(wq_ref, wq_s, w_sem.at[0]),
        pltpu.make_async_copy(wk_ref, wk_s, w_sem.at[1]),
        pltpu.make_async_copy(wv_ref, wv_s, w_sem.at[2]),
    ]

    def o_copy(t):
        col = pl.multiple_of(lax.rem(me + t, ways) * feats, LANES)
        return pltpu.make_async_copy(wo_ref.at[:, pl.ds(col, feats)], wo_s.at[t], o_sem.at[t])

    def kv_copy(r, j):
        return pltpu.make_async_copy(
            cache_ref.at[table_ref[0, j, r]],
            kv_s.at[r, :, :, pl.ds(0, HEAD_DIM), pl.ds(j * block_len, block_len)],
            kv_sem.at[r * per + j],
        )

    for t in range(ways):
        x_copy(t).start()
    for copy in w_copies:
        copy.start()

    def kv_start(r, carry):
        for j in range(per):
            kv_copy(r, j).start()
        return carry

    lax.fori_loop(0, reqs, kv_start, 0)
    for t in range(ways):
        o_copy(t).start()

    row_id = lax.broadcasted_iota(jnp.int32, (rows, LANES), 0)

    def shift_of(r, carry):
        offset, shift = carry
        shift = jnp.where(row_id >= offset, lens_ref[0, r] - offset, shift)
        return offset + span_ref[0, r], shift

    _, shift = lax.fori_loop(0, reqs, shift_of, (jnp.int32(0), jnp.zeros_like(row_id)))
    angle = (row_id + shift).astype(jnp.float32) * inv_ref[...]
    lane = lax.broadcasted_iota(jnp.int32, (rows, LANES), 1)
    cos_s[...] = jnp.where(lane < HEAD_DIM, jnp.cos(angle), 0.0)
    sine = jnp.sin(angle)
    low_s[...] = jnp.where(lane < HALF, -sine, 0.0)
    high_s[...] = jnp.where((lane >= HALF) & (lane < HEAD_DIM), sine, 0.0)

    pad = kv_s.shape[3] - HEAD_DIM
    zeros_kv = jnp.zeros((2, pad, kv_s.shape[4]), kv_s.dtype)

    def kv_zero(r, carry):
        for g in range(kv_heads):
            kv_s[r, g, :, HEAD_DIM:, :] = zeros_kv
        return carry

    lax.fori_loop(0, reqs, kv_zero, 0)
    acc_s[...] = jnp.zeros(acc_s.shape, acc_s.dtype)

    for t in range(ways):
        x_copy(t).wait()
    step = 64

    def norm_rows(m, carry):
        here = pl.ds(pl.multiple_of(m * step, step), step)
        wide = [x_s[t, here, :].astype(jnp.float32) for t in range(ways)]
        total = sum(jnp.sum(w * w, axis=1, keepdims=True) for w in wide)
        scale = lax.rsqrt(total / (ways * feats) + EPS)
        for t in range(ways):
            nrm_s[lax.rem(me + t, ways), here, :] = (
                wide[t] * scale * gains[t][...].astype(jnp.float32)
            ).astype(jnp.bfloat16)
        return carry

    lax.fori_loop(0, rows // step, norm_rows, 0)

    tall = 256

    def project(w_s, first, width, here):
        total = None
        for c in range(ways):
            deep = slice(c * feats, (c + 1) * feats)
            if first is None:
                part = lax.dot_general(
                    nrm_s[c, here, :], w_s[:, deep], NT, preferred_element_type=jnp.float32
                )
            else:
                part = jnp.dot(
                    nrm_s[c, here, :], w_s[deep, first : first + width],
                    preferred_element_type=jnp.float32,
                )
            total = part if total is None else total + part
        acc_s[:, :width] = total

    def head_of(h):
        base = HEAD_DIM * h // LANES * LANES
        shift = HEAD_DIM * h - base
        wide = acc_s[:, base : base + 2 * LANES]
        if shift:
            wide = pltpu.roll(wide, 2 * LANES - shift, 1)
        return wide[:, :LANES]

    def rotated(h, here):
        value = head_of(h)
        return (
            value * cos_s[here, :]
            + pltpu.roll(value, LANES - HALF, 1) * low_s[here, :]
            + pltpu.roll(value, HALF, 1) * high_s[here, :]
        ).astype(jnp.bfloat16)

    for copy in w_copies:
        copy.wait()
    block_heads = min(8, q_heads)

    def project_rows(m, carry):
        here = pl.ds(pl.multiple_of(m * tall, tall), tall)
        project(wk_s, None, kv_heads * HEAD_DIM, here)
        for g in range(kv_heads):
            k_s[g, here, :] = rotated(g, here)
        project(wv_s, None, kv_heads * HEAD_DIM, here)
        narrow = lax.broadcasted_iota(jnp.int32, (tall, LANES), 1) < HEAD_DIM
        for g in range(kv_heads):
            v_s[g, here, :] = jnp.where(narrow, head_of(g), 0.0).astype(jnp.bfloat16)
        for block in range(q_heads // block_heads):
            project(wq_s, block * block_heads * HEAD_DIM, block_heads * HEAD_DIM, here)
            for h in range(block_heads):
                q_s[block * block_heads + h, here, :] = rotated(h, here)
        return carry

    lax.fori_loop(0, rows // tall, project_rows, 0)

    log_scale = (1.0 / math.sqrt(HEAD_DIM)) * math.log2(math.e)
    keys_old = per * block_len

    def request(r, offset):
        span = span_ref[0, r]
        prior = lens_ref[0, r]
        for j in range(per):
            kv_copy(r, j).wait()
        first = offset // 16 * 16
        key_first = pl.multiple_of(jnp.minimum(first, rows - LANES), 16)
        old_ok = lax.broadcasted_iota(jnp.int32, (1, keys_old), 1) < prior

        def tile(i, carry):
            begin = pl.multiple_of(first + i * ROWS, 16)
            here = pl.ds(begin, ROWS)
            row = begin + lax.broadcasted_iota(jnp.int32, (ROWS, LANES), 0)
            key = key_first + lax.broadcasted_iota(jnp.int32, (ROWS, LANES), 1)
            new_ok = ((key <= row) & (key >= offset))[None]
            keep = ((row >= offset) & (row < offset + span))[None]
            scores = []
            for g in range(kv_heads):
                heads = slice(g * group, (g + 1) * group)
                query = q_s[heads, here, :].reshape(group * ROWS, LANES)
                old = jnp.dot(query, kv_s[r, g, 0], preferred_element_type=jnp.float32)
                new = lax.dot_general(
                    query, k_s[g, pl.ds(key_first, LANES), :], NT,
                    preferred_element_type=jnp.float32,
                )
                scores.append((old, new))
            probs = []
            for old, new in scores:
                old = jnp.where(old_ok, old, MASKED)
                new = jnp.where(new_ok, new.reshape(group, ROWS, LANES), MASKED)
                new = new.reshape(group * ROWS, LANES)
                wide = jnp.maximum(jnp.maximum(old[:, :LANES], old[:, LANES:]), new)
                top = jnp.max(wide, axis=1, keepdims=True)
                old = jnp.exp2((old - top) * log_scale)
                new = jnp.exp2((new - top) * log_scale)
                wide = old[:, :LANES] + old[:, LANES:] + new
                total = jnp.sum(wide, axis=1, keepdims=True)
                probs.append((old.astype(jnp.bfloat16), new.astype(jnp.bfloat16), total))
            for g in range(kv_heads):
                heads = slice(g * group, (g + 1) * group)
                old, new, total = probs[g]
                mixed = lax.dot_general(
                    old, kv_s[r, g, 1], NT, preferred_element_type=jnp.float32,
                ) + jnp.dot(
                    new, v_s[g, pl.ds(key_first, LANES), :],
                    preferred_element_type=jnp.float32,
                )
                mixed = (mixed / total).reshape(group, ROWS, LANES)
                att_s[heads, here, :] = jnp.where(keep, mixed, att_s[heads, here, :])
            return carry

        lax.fori_loop(0, (offset - first + span + ROWS - 1) // ROWS, tile, 0)
        return offset + span

    lax.fori_loop(0, reqs, request, jnp.int32(0))

    for t in range(ways):
        o_copy(t).wait()

    def out_rows(m, carry):
        here = pl.ds(pl.multiple_of(m * tall, tall), tall)
        flat_s[...] = jnp.zeros(flat_s.shape, flat_s.dtype)
        for h in range(q_heads):
            base = HEAD_DIM * h // LANES * LANES
            shift = HEAD_DIM * h - base
            value = att_s[h, here, :]
            wide = jnp.concatenate([value, jnp.zeros_like(value)], axis=1)
            if shift:
                wide = pltpu.roll(wide, shift, 1)
            flat_s[:, base : base + 2 * LANES] += wide
        flat = flat_s[:, : q_heads * HEAD_DIM].astype(jnp.bfloat16)
        for t in range(ways):
            part = jnp.dot(flat, wo_s[t], preferred_element_type=jnp.float32)
            if t == 0:
                base_ref[here, :] = x_s[0, here, :].astype(jnp.float32) + part
            else:
                sends[t - 1][here, :] = part.astype(jnp.bfloat16)
        return carry

    lax.fori_loop(0, rows // tall, out_rows, 0)


def layer(ways, spans, lens, table, gains, xs, w_query, w_key, w_value, w_out, cache):
    rows, feats = xs[0].shape
    q_heads = w_query.shape[1] // HEAD_DIM
    kv_heads = w_key.shape[0] // HEAD_DIM
    per, reqs = table.shape[1], table.shape[2]
    keys = per * cache.shape[-1]
    pairs = np.arange(LANES) % HALF
    inverse = np.where(
        np.arange(LANES) < HEAD_DIM, np.float64(THETA) ** (-2.0 * pairs / HEAD_DIM), 0.0
    ).astype(np.float32)[None]
    bf, f32 = jnp.bfloat16, jnp.float32
    outs = pl.pallas_call(
        functools.partial(layer_body, ways, q_heads, kv_heads),
        out_shape=[jax.ShapeDtypeStruct((rows, feats), f32)]
        + [jax.ShapeDtypeStruct((rows, feats), bf)] * (ways - 1),
        in_specs=[smem(), smem(), smem(), vmem()] + [vmem()] * ways + [hbm()] * (ways + 5),
        out_specs=[vmem()] * ways,
        scratch_shapes=[
            pltpu.VMEM((ways, rows, feats), bf),
            pltpu.VMEM((ways, rows, feats), bf),
            pltpu.VMEM(w_query.shape, bf),
            pltpu.VMEM(w_key.shape, bf),
            pltpu.VMEM(w_value.shape, bf),
            pltpu.VMEM((ways, w_out.shape[0], feats), bf),
            pltpu.VMEM((reqs, kv_heads, 2, LANES, keys), bf),
            pltpu.VMEM((256, min(8, q_heads) * HEAD_DIM + LANES), f32),
            pltpu.VMEM((q_heads, rows + ROWS, LANES), bf),
            pltpu.VMEM((kv_heads, rows, LANES), bf),
            pltpu.VMEM((kv_heads, rows, LANES), bf),
            pltpu.VMEM((q_heads, rows + ROWS, LANES), f32),
            pltpu.VMEM((256, q_heads * HEAD_DIM + LANES), f32),
            pltpu.VMEM((rows, LANES), f32),
            pltpu.VMEM((rows, LANES), f32),
            pltpu.VMEM((rows, LANES), f32),
            pltpu.SemaphoreType.DMA((ways,)),
            pltpu.SemaphoreType.DMA((3,)),
            pltpu.SemaphoreType.DMA((ways,)),
            pltpu.SemaphoreType.DMA((reqs * per,)),
        ],
        compiler_params=pltpu.CompilerParams(vmem_limit_bytes=LAYER_VMEM),
        cost_estimate=pl.CostEstimate(
            flops=100 * 2 * rows * ways * feats * 2 * w_query.shape[1],
            transcendentals=0,
            bytes_accessed=4 * w_query.size,
        ),
        name="layer",
    )(spans, lens, table, jnp.asarray(inverse), *gains, *xs, w_query, w_key, w_value, w_out, cache)
    return outs[0], outs[1:]


def local(
    tokens,
    norm_gain,
    w_query,
    w_key,
    w_value,
    w_out,
    prior_cache,
    prior_lens,
    span_lens,
    prior_table,
    dest_device,
    dest_table,
):
    ways = lax.axis_size("tp")
    w_key, w_value = w_key.T, w_value.T
    prior_table = prior_table.transpose(0, 2, 1)
    dest_table = dest_table.transpose(0, 2, 1)
    def from_peer(value, t):
        return lax.ppermute(value, "tp", [((d + t) % ways, d) for d in range(ways)])

    def to_peer(value, t):
        return lax.ppermute(value, "tp", [(d, (d + t) % ways) for d in range(ways)])

    peers = lax.axis_size("seq")
    pairs = peers // 2

    def to_hop(value, hop):
        return lax.ppermute(value, "seq", [(d, d ^ hop) for d in range(peers)])

    barrier = lax.optimization_barrier
    far = list(range(pairs // 2, pairs))
    near = list(range(1, pairs // 2))
    pair = lambda k: (2 * k, 2 * k + 1)
    begin = far[:2] + near[:1]
    middle = near[1:]
    late = [hop for k in far[2:] for hop in pair(k)]
    args = (dest_device, prior_lens, prior_table, prior_cache)
    heads = prior_cache.shape[1]
    few = max(1, heads * BY_PERMUTE // 4)
    xs = [tokens] + [from_peer(tokens, t) for t in range(1, ways)]
    begin_out = pack([pair(k) for k in begin], *args, [], 0, few)
    (bulk_out,) = pack(
        [tuple(range(peers))], *args, begin_out[-1:], few, heads - few, absolute=True
    )
    hops = [pair(k) for k in middle] + [(hop,) for hop in late] + [(0, 1)]
    rest = pack(hops, *args, [bulk_out], 0, few)
    middle_out, late_out, own = rest[: len(middle)], rest[len(middle) : -1], rest[-1]
    begin_in = [to_hop(value, 2 * k) for k, value in zip(begin, begin_out)]
    bulk_in = lax.all_to_all(bulk_out, "seq", split_axis=0, concat_axis=0, tiled=True)
    gain = barrier((norm_gain, bulk_out))[0][None, :]
    gains = [gain] + [from_peer(gain, t) for t in range(1, ways)]
    xs, begin_in = barrier((xs, begin_in))
    base, sends = layer(
        ways, span_lens, prior_lens, prior_table, gains, xs,
        w_query, w_key, w_value, w_out, prior_cache,
    )
    sends, middle_out, late_out = barrier((sends, middle_out, late_out))
    middle_in = [to_hop(value, 2 * k) for k, value in zip(middle, middle_out)]
    late_in = [to_hop(value, hop) for hop, value in zip(late, late_out)]
    got = [to_peer(sends[t - 1], t) for t in range(1, ways)]
    arrived = begin_in + middle_in
    other = to_hop(relay(arrived + [own], got), 1)
    reach = [2 * k for k in begin + middle] + [0]
    sources = [(i, 0, hop) for i, hop in enumerate(reach)]
    sources += [(len(reach), i, hop + 1) for i, hop in enumerate(reach)]
    shape = prior_cache.shape
    got, other = barrier((got, other))
    total = base
    for value in got:
        total = total + value.astype(jnp.float32)
    hidden = total.astype(jnp.bfloat16)
    made = place(dest_table, arrived + [own, other], sources, shape, 0)
    bulk = [(0, s, s) for s in range(peers)]
    made = place(dest_table, [bulk_in], bulk, shape, few, [made], absolute=True)
    decode_cache = place_last(dest_table, late_in, late, made)
    return (hidden, decode_cache)


def solution(mesh):
    in_specs = (
        P("seq", "tp"),
        P("tp"),
        P(None, "tp"),
        P(None, "tp"),
        P(None, "tp"),
        P("tp", None),
        P("seq", "tp", None, None, None),
        P("seq", None),
        P("seq", None),
        P("seq", None, None),
        P("seq", None),
        P("seq", None, None),
    )
    out_specs = (P("seq", "tp"), P("seq", "tp", None, None, None))
    return jax.shard_map(local, mesh=mesh, in_specs=in_specs, out_specs=out_specs, check_vma=False)
```
